32 devices in a mesh: item: 2 (over core), site: 16 (over z, y, x).
Axes of the slice: x: 2, y: 2, z: 4, core: 2. Of those that a mesh axis runs over, the one named last changes fastest.
Arguments:
- item_factors: float32 [16, 32, 65536], P('site', None, 'item'), may hold values from -3 to 3
- user_factors: float32 [16, 32, 4096], P('site', None, 'item'), may hold values from -3 to 3
- ratings: bfloat16 [16, 2, 128, 128, 128], P('site', 'item'), may hold values from -6 to 6
- block_rows: int32 [16, 2, 128], P('site', 'item'), may hold values from 0 to 255, as said below
- block_cols: int32 [16, 2, 128], P('site', 'item'), may hold values from 0 to 31
- block_count: int32 [16, 2], P('site', 'item'), may hold values from 16 to 128, as said below
- hop_steps: int32 [2], replicated, may hold values from 0 to 2, as said below
Outputs:
- items_out: float32 [16, 32, 65536], P('site', None, 'item')
- users_out: float32 [16, 32, 4096], P('site', None, 'item')
The draws below stay inside these ranges and needn't reach their ends.
Inputs may be any that keep to these rules, and one draw needn't show every extreme that they name: `block_rows`: within one device the live and empty slots name distinct pairs of blocks. `block_count`: some device has all 128 slots live. `hop_steps`: the steps' exponents differ.
All inputs are finite; a program needn't handle non-finite values.
Results may differ from the reference program's by a relative error of at most 0.0003.
Values sent between devices are 32-bit elements; how exact they have to be, the bound alone decides.
A program may use at most 128 MiB of HBM per device.

```python
import jax
import jax.numpy as jnp
from jax import lax

ITEMS = 65536
R = 32
BLK = 128
NB = 128
ITERS = 2
ITEM_DEV = 32768
USERS = 4096
ROW_BLOCKS = 256
COL_BLOCKS = 32
N_ITEM = 2
N_SITE = 16


def block_pairs(key):
    device_keys = jax.random.split(jax.random.fold_in(key, 17), N_SITE * N_ITEM)

    def device_pairs(device_key):
        return jax.random.permutation(device_key, ROW_BLOCKS * COL_BLOCKS)[:NB]
    paired = jax.vmap(device_pairs)(device_keys).astype(jnp.int32)
    return paired.reshape(N_SITE, N_ITEM, NB)


def draw_block_rows(key, part):
    return (block_pairs(key) // COL_BLOCKS).astype(jnp.int32)


def draw_block_cols(key, part):
    return (block_pairs(key) % COL_BLOCKS).astype(jnp.int32)


def draw_block_count(key, part):
    shrink = jax.random.randint(jax.random.fold_in(key, 5), (N_SITE * N_ITEM,), 0, 4)
    totals = NB // jnp.left_shift(jnp.int32(1), shrink.astype(jnp.int32))
    busiest = jax.random.randint(jax.random.fold_in(key, 9), (), 0, N_SITE * N_ITEM)
    totals = totals.at[busiest].set(NB)
    return totals.reshape(N_SITE, N_ITEM).astype(jnp.int32)


def draw_hop_steps(key, part):
    exponents = jnp.array([0, 2, 1], dtype=jnp.int32)[:ITERS]
    return jax.random.permutation(jax.random.fold_in(key, 3), exponents).astype(jnp.int32)


def level_of(stream_key, dims, shards, least, top_value):
    def one(dim, shards_of):
        draws = jax.random.uniform(jax.random.fold_in(jax.random.fold_in(stream_key, 6), dim), (shards_of,), jnp.float32, least / len(shards), top_value / len(shards))
        return jnp.repeat(jnp.exp(draws), dims[dim] // shards_of).reshape((-1,) + (1,) * (len(dims) - dim - 1))

    factor_of = one(*shards[0])
    for cut in shards[1:]:
        factor_of = factor_of * one(*cut)
    return factor_of


def gaussian(own_key, shape, scale, most, cuts=(), kind=jnp.bfloat16):
    result = jax.random.normal(own_key, shape, jnp.float32) * scale
    if len(cuts) > 0:
        result = level_of(own_key, shape, cuts, -0.22, 0.18) * result
    return jnp.clip(result, min=-most, max=most).astype(kind)


def setup_inputs(seed: int = 0) -> dict:
    seeds = jax.random.split(jax.random.key(seed), 8)
    return {
        "item_factors": gaussian(seeds[0], (N_SITE, R, ITEMS), 0.5, 3.0, ((0, 16), (2, 2)), jnp.float32),
        "user_factors": gaussian(seeds[1], (N_SITE, R, USERS), 0.5, 3.0, ((0, 16), (2, 2)), jnp.float32),
        "ratings": gaussian(seeds[2], (N_SITE, N_ITEM, NB, BLK, BLK), 1.0, 6.0, ((0, 16), (1, 2))),
        "block_rows": draw_block_rows(jax.random.fold_in(seeds[7], 71), 0),
        "block_cols": draw_block_cols(jax.random.fold_in(seeds[7], 71), 0),
        "block_count": draw_block_count(jax.random.fold_in(seeds[7], 71), 0),
        "hop_steps": draw_hop_steps(jax.random.fold_in(seeds[7], 71), 0),
    }


LEARN_RATE = 0.05


def shard_grads(item_shard, user_site, slot_values, row_index, column_index, block_total):
    item_tiles = item_shard.reshape(R, ROW_BLOCKS, BLK)
    user_tiles = user_site.reshape(R, COL_BLOCKS, BLK)
    item_picked = jnp.transpose(item_tiles[:, row_index, :], (1, 0, 2))
    user_picked = jnp.transpose(user_tiles[:, column_index, :], (1, 0, 2))
    rebuilt = jnp.einsum("nri,nrj->nij", item_picked, user_picked, precision=lax.Precision.HIGHEST)
    live_mask = (jnp.arange(NB, dtype=jnp.int32) < block_total).astype(jnp.float32)
    clipped = jnp.clip(rebuilt - slot_values.astype(jnp.float32), -1.0, 1.0) * live_mask[:, None, None]
    item_part = jnp.einsum("nij,nrj->nri", clipped, user_picked, precision=lax.Precision.HIGHEST)
    user_part = jnp.einsum("nij,nri->nrj", clipped, item_picked, precision=lax.Precision.HIGHEST)
    item_grad = jnp.zeros((ROW_BLOCKS, R, BLK), jnp.float32).at[row_index].add(item_part)
    user_grad = jnp.zeros((COL_BLOCKS, R, BLK), jnp.float32).at[column_index].add(user_part)
    item_grad = jnp.transpose(item_grad, (1, 0, 2)).reshape(R, ITEM_DEV)
    user_grad = jnp.transpose(user_grad, (1, 0, 2)).reshape(R, USERS)
    return item_grad, user_grad


def site_grads(packed):
    item_site, user_site, slot_values, row_index, column_index, block_total = packed
    item_shards = jnp.transpose(item_site.reshape(R, N_ITEM, ITEM_DEV), (1, 0, 2))
    item_grad, user_grad = jax.vmap(shard_grads, in_axes=(0, None, 0, 0, 0, 0))(
        item_shards, user_site, slot_values, row_index, column_index, block_total)
    item_grad = jnp.transpose(item_grad, (1, 0, 2)).reshape(R, ITEMS)
    return item_grad, jnp.sum(user_grad, axis=0)


def reference(item_factors, user_factors, ratings, block_rows, block_cols, block_count, hop_steps):
    item_state = item_factors
    user_state = user_factors
    for step_index in range(ITERS):
        item_grad, user_grad = lax.map(site_grads, (item_state, user_state, ratings, block_rows, block_cols, block_count))
        peer_hop = jnp.left_shift(jnp.int32(1), hop_steps[step_index].astype(jnp.int32))
        peer_items = jnp.roll(item_state, -peer_hop, axis=0)
        item_state = 0.5 * (item_state + peer_items) - LEARN_RATE * item_grad
        user_state = user_state - LEARN_RATE * user_grad
    return item_state, user_state
```

```python
from functools import partial

import jax
import jax.numpy as jnp
from jax import lax
from jax.experimental import pallas as pl
from jax.experimental.pallas import tpu as pltpu
from jax.sharding import PartitionSpec as P

ITERS = 2
HOPS = 3
LEARN_RATE = 0.05
CHUNKS = 4
GROUP = 8
RELAYS = 4
KERNEL_WEIGHT = 450
PIECES = 8
HALVES = 2
BLEND_GROUP = 8
BLEND_STEPS = 8


def passed_along(block, axis, distance):
    devices = range(lax.axis_size(axis))
    route = [((i - distance) % len(devices), i) for i in devices]
    return lax.ppermute(block, axis, route)


def split_high_low(values):
    high = values.astype(jnp.bfloat16)
    low = (values - high.astype(jnp.float32)).astype(jnp.bfloat16)
    return high, low


def dot_f32(lhs, rhs, lhs_dim, rhs_dim):
    return lax.dot_general(
        lhs, rhs, (((lhs_dim,), (rhs_dim,)), ((), ())), preferred_element_type=jnp.float32
    )


def grads_kernel(chunks, rows_ref, cols_ref, count_ref, *refs):
    x_refs = refs[:chunks]
    y_ref, ratings_ref = refs[chunks : chunks + 2]
    base_ref, user_ref = refs[chunks + 2 :]
    group, tile = ratings_ref.shape[0], ratings_ref.shape[-1]
    rank = y_ref.shape[0]
    first = pl.program_id(0) * group
    total = count_ref[0]

    @pl.when(pl.program_id(0) == 0)
    def _():
        start = 0
        for x_ref in x_refs:
            base_ref[start : start + x_ref.shape[0], :] = 0.5 * x_ref[...]
            start += x_ref.shape[0]
        user_ref[...] = jnp.zeros_like(user_ref)

    @pl.when(first < total)
    def _():
        parts = []
        for k in range(group):
            row = pl.ds(pl.multiple_of(rows_ref[first + k] * tile, tile), tile)
            col = pl.ds(pl.multiple_of(cols_ref[first + k] * tile, tile), tile)
            limit = jnp.where(first + k < total, 1.0, 0.0).astype(jnp.float32)
            x = jnp.concatenate([x_ref[:, row] for x_ref in x_refs], axis=0)
            x_high, x_low = split_high_low(x)
            y_high, y_low = split_high_low(y_ref[:, col])
            rebuilt = dot_f32(
                jnp.concatenate([x_high, x_low, x_high], axis=0),
                jnp.concatenate([y_high, y_high, y_low], axis=0),
                0,
                0,
            )
            clipped = jnp.clip(rebuilt - ratings_ref[k].astype(jnp.float32), -limit, limit)
            c_high, c_low = split_high_low(clipped)
            item_pair = dot_f32(jnp.concatenate([y_high, y_low], axis=0), c_high, 1, 1)
            item_part = item_pair[:rank] + item_pair[rank:] + dot_f32(y_high, c_low, 1, 1)
            user_pair = dot_f32(jnp.concatenate([x_high, x_low], axis=0), c_high, 1, 0)
            user_part = user_pair[:rank] + user_pair[rank:] + dot_f32(x_high, c_low, 1, 0)
            parts.append((row, col, item_part, user_part))
        for row, col, item_part, user_part in parts:
            base_ref[:, row] -= LEARN_RATE * item_part
            user_ref[:, col] += user_part


def local_grads(x_parts, users_whole, slot_values, row_index, column_index, block_total):
    chunks = len(x_parts)
    slot_total, tile = slot_values.shape[0], slot_values.shape[-1]
    rank, users = users_whole.shape
    items = x_parts[0].shape[1]
    once = pl.Buffered(1)
    held = lambda shape: pl.BlockSpec(shape, lambda i, *_: (0, 0), pipeline_mode=once)
    return pl.pallas_call(
        partial(grads_kernel, chunks),
        grid_spec=pltpu.PrefetchScalarGridSpec(
            num_scalar_prefetch=3,
            grid=(slot_total // GROUP,),
            in_specs=[held(part.shape) for part in x_parts]
            + [held((rank, users)), pl.BlockSpec((GROUP, tile, tile), lambda i, *_: (i, 0, 0))],
            out_specs=[held((rank, items)), held((rank, users))],
        ),
        out_shape=[
            jax.ShapeDtypeStruct((rank, items), jnp.float32),
            jax.ShapeDtypeStruct((rank, users), jnp.float32),
        ],
        compiler_params=pltpu.CompilerParams(vmem_limit_bytes=24 << 20),
        cost_estimate=pl.CostEstimate(
            flops=KERNEL_WEIGHT * slot_total * tile * tile * rank,
            bytes_accessed=8 * rank * items + 2 * slot_total * tile * tile,
            transcendentals=0,
        ),
    )(row_index, column_index, block_total, *x_parts, users_whole, slot_values)


def over_items(block):
    total = block
    for distance in range(1, lax.axis_size("item")):
        total = total + passed_along(block, "item", distance)
    return total


def owned_part(whole):
    count = lax.axis_size("item")
    width = whole.shape[1] // count
    me = lax.axis_index("item")
    cut = lambda who: lax.dynamic_slice_in_dim(whole, who * width, width, axis=1)
    total = cut(me)
    for distance in range(1, count):
        total = total + passed_along(cut(lax.rem(me + distance, count)), "item", distance)
    return total


def kept_part(whole):
    width = whole.shape[1] // lax.axis_size("item")
    return lax.dynamic_slice_in_dim(whole, lax.axis_index("item") * width, width, axis=1)


def blend_kernel(base_ref, *refs):
    out_ref = refs[-1]
    start = 0
    for ref in refs[:-1]:
        rows = slice(start, start + ref.shape[0])
        out_ref[rows, :] = base_ref[rows, :] + 0.5 * ref[...]
        start += ref.shape[0]


def blend(base, peers):
    rank, items = base.shape
    width = items // BLEND_STEPS
    spec = lambda rows: pl.BlockSpec((rows, width), lambda i: (0, i))
    return pl.pallas_call(
        blend_kernel,
        grid=(BLEND_STEPS,),
        in_specs=[spec(rank)] + [spec(peer.shape[0]) for peer in peers],
        out_specs=spec(rank),
        out_shape=jax.ShapeDtypeStruct((rank, items), jnp.float32),
    )(base, *peers)


def cut_rows(block):
    size = block.shape[0] // CHUNKS
    return [block[c * size : (c + 1) * size] for c in range(CHUNKS)]


def two_steps(hops, item_here, user_here, slot_values, row_index, column_index, block_total):
    grads = lambda parts, users: local_grads(
        parts, users, slot_values, row_index, column_index, block_total
    )
    peers = [passed_along(part, "site", -(1 << hops[0])) for part in cut_rows(item_here)]
    users_whole = lax.all_gather(user_here, "item", axis=1, tiled=True)
    base, user_grad = grads([item_here], users_whole)
    users_whole = users_whole - LEARN_RATE * over_items(user_grad)
    x_parts = [part + 0.5 * peer for part, peer in zip(cut_rows(base), peers)]
    peers = [passed_along(part, "site", -(1 << hops[1])) for part in x_parts]
    base, user_grad = grads(x_parts, users_whole)
    return blend(base, peers), kept_part(users_whole) - LEARN_RATE * owned_part(user_grad)


def slot_index(row_index, column_index, row_blocks, column_blocks):
    slots = row_index.shape[0]
    order = jnp.arange(slots, dtype=jnp.int32)

    def latest(wanted, keys, limit):
        hit = jnp.logical_and(wanted[:, None] == keys[None, :], order[None, :] < limit[:, None])
        found = jnp.max(jnp.where(hit, order[None, :], -1), axis=1)
        return jnp.where(found < 0, slots, found)

    def both(keys, blocks):
        wanted = jnp.concatenate([keys, jnp.arange(blocks, dtype=jnp.int32)])
        limit = jnp.concatenate([order, jnp.full((blocks,), slots, jnp.int32)])
        return latest(wanted, keys, limit)

    return jnp.concatenate(
        [row_index, column_index, both(row_index, row_blocks), both(column_index, column_blocks)]
    )


def fused_kernel(hops, index_ref, live_ref, x_in, y_in, ratings_in, x_out, y_out, *refs):
    x, x1, land_a, land_b, relay_a, relay_b, ratings, item_sum, user_sum = refs[:9]
    y, grad, grad_land, part_land, x_tiles, y_tiles = refs[9:15]
    send_a, recv_a, send_b, recv_b, take_a, give_a, take_b, give_b, swaps, loads = refs[15:]
    site, item = lax.axis_index("site"), lax.axis_index("item")
    sites = lax.axis_size("site")
    place = lax.rem(site, RELAYS)
    layer = site - place
    last = RELAYS - 1
    ahead = lax.rem(site + sites - RELAYS, sites)
    behind = lax.rem(site + RELAYS, sites)
    ahead_layer, behind_layer = ahead - place, behind - place
    rank, items = x.shape
    own = y_in.shape[1]
    users = y.shape[1]
    slots, tile = ratings.shape[0], ratings.shape[-1]
    row_blocks, column_blocks = items // tile, users // tile
    pieces = PIECES
    rows = rank // (pieces // HALVES)
    width = items // HALVES
    part = width // RELAYS
    at_rows, at_cols = 0, slots
    at_row_prev = 2 * slots
    at_row_last = at_row_prev + slots
    at_col_prev = at_row_last + row_blocks
    at_col_last = at_col_prev + slots

    def spot(j):
        return (j // HALVES) * rows, (j % HALVES) * width

    def view(ref, j):
        r, c = spot(j)
        return ref.at[pl.ds(r, rows), pl.ds(c, width)]

    def slab(ref, j, q):
        r, c = spot(j)
        return ref.at[pl.ds(r, rows), pl.ds(c + q * part, part)]

    def copy(src, dst, send, recv, target):
        return pltpu.make_async_remote_copy(
            src_ref=src,
            dst_ref=dst,
            send_sem=send,
            recv_sem=recv,
            device_id=(item, target),
            device_id_type=pl.DeviceIdType.MESH,
        )

    def to_partner(src, dst, k):
        return pltpu.make_async_remote_copy(
            src_ref=src,
            dst_ref=dst,
            send_sem=swaps.at[2 * k],
            recv_sem=swaps.at[2 * k + 1],
            device_id=(1 - item, site),
            device_id_type=pl.DeviceIdType.MESH,
        )

    flows = (
        (hops[0], x_in, land_a, relay_a, send_a, recv_a, take_a, give_a),
        (hops[1], x1, land_b, relay_b, send_b, recv_b, take_b, give_b),
    )

    def send(flow, j):
        hop, src, land, relay, send_sem, recv_sem, take, give = flows[flow]
        if hop != 0:
            copy(view(src, j), view(land, j), send_sem.at[j], recv_sem.at[j], ahead).start()
            return

        @pl.when(place != 0)
        def _():
            copy(view(src, j), view(land, j), send_sem.at[j], recv_sem.at[j], site - 1).start()

        @pl.when(place == 0)
        def _():
            for q in range(last, 0, -1):
                copy(slab(src, j, q), relay.at[j], send_sem.at[j], take.at[j], site + q).start()
            copy(
                slab(src, j, 0), slab(land, j, 0), send_sem.at[j], recv_sem.at[j], ahead + last
            ).start()

    def forward(flow, j):
        hop, src, land, relay, send_sem, recv_sem, take, give = flows[flow]
        if hop != 0:
            return
        for q in range(1, RELAYS):

            @pl.when(place == q)
            def _():
                out = copy(
                    relay.at[j], slab(land, j, q), give.at[j], recv_sem.at[j], ahead_layer + last
                )
                copy(relay.at[j], relay.at[j], give.at[j], take.at[j], ahead).wait_recv()
                out.start()

    def forwarded(flow, j):
        hop, src, land, relay, send_sem, recv_sem, take, give = flows[flow]
        if hop != 0:
            return

        @pl.when(place != 0)
        def _():
            copy(relay.at[j], relay.at[j], give.at[j], take.at[j], ahead).wait_send()

    def waiter(flow, j):
        hop, src, land, relay, send_sem, recv_sem, take, give = flows[flow]
        return copy(view(src, j), view(land, j), send_sem.at[j], recv_sem.at[j], ahead)

    barrier = pltpu.get_barrier_semaphore()

    def greet(core, peer):
        pl.semaphore_signal(
            barrier, inc=1, device_id=(core, peer), device_id_type=pl.DeviceIdType.MESH
        )

    for k in range(1, RELAYS):
        greet(item, layer + lax.rem(place + k, RELAYS))
    greet(item, ahead)
    greet(item, behind)
    greet(1 - item, site)

    @pl.when(place != last)
    def _():
        greet(item, ahead_layer + last)
        pl.semaphore_wait(barrier, RELAYS + 3)

    @pl.when(place == last)
    def _():
        for q in range(last):
            greet(item, behind_layer + q)
        pl.semaphore_wait(barrier, RELAYS + 2 + last)

    mine = pl.ds(pl.multiple_of(item * own, own), own)
    swap = to_partner(y_in, y.at[:, mine], 0)
    swap.start()
    for j in range(pieces):
        send(0, j)
    take_x = pltpu.make_async_copy(x_in, x, loads.at[0])
    take_y = pltpu.make_async_copy(y_in, y.at[:, mine], loads.at[1])
    take_ratings = pltpu.make_async_copy(ratings_in, ratings, loads.at[2])
    take_x.start()
    take_y.start()
    take_ratings.start()
    item_sum[slots] = jnp.zeros((rank, tile), jnp.float32)
    user_sum[slots] = jnp.zeros((rank, tile), jnp.float32)
    take_x.wait()
    take_y.wait()
    swap.wait()
    take_ratings.wait()

    def tiled(src, dst):
        def body(c, carry):
            dst[c] = src[:, pl.ds(pl.multiple_of(c * tile, tile), tile)]
            return carry

        lax.fori_loop(0, dst.shape[0], body, 0, unroll=8)

    def grad_group(first):
        parts = []
        for k in range(GROUP):
            slot = first + k
            limit = live_ref[slot]
            x_high, x_low = split_high_low(x_tiles[index_ref[at_rows + slot]])
            y_high, y_low = split_high_low(y_tiles[index_ref[at_cols + slot]])
            rebuilt = dot_f32(
                jnp.concatenate([x_high, x_low, x_high], axis=0),
                jnp.concatenate([y_high, y_high, y_low], axis=0),
                0,
                0,
            )
            clipped = jnp.clip(rebuilt - ratings[slot].astype(jnp.float32), -limit, limit)
            c_high, c_low = split_high_low(clipped)
            item_pair = dot_f32(jnp.concatenate([y_high, y_low], axis=0), c_high, 1, 1)
            item_part = item_pair[:rank] + item_pair[rank:] + dot_f32(y_high, c_low, 1, 1)
            user_pair = dot_f32(jnp.concatenate([x_high, x_low], axis=0), c_high, 1, 0)
            user_part = user_pair[:rank] + user_pair[rank:] + dot_f32(x_high, c_low, 1, 0)
            parts.append((slot, item_part, user_part))
        for slot, item_part, user_part in parts:
            item_sum[slot] = item_part + item_sum[index_ref[at_row_prev + slot]]
            user_sum[slot] = user_part + user_sum[index_ref[at_col_prev + slot]]

    def grads(start, stop):
        def body(g, carry):
            grad_group(g * GROUP)
            return carry

        lax.fori_loop(start, stop, body, 0)

    def collect():
        def body(c, carry):
            at = pl.ds(pl.multiple_of(c * tile, tile), tile)
            grad[:, at] = user_sum[index_ref[at_col_last + c]]
            return carry

        lax.fori_loop(0, column_blocks, body, 0)

    def blend(old, land, out, j, tiles=None):
        r, c = spot(j)
        band = slice(r, r + rows)

        def body(g, carry):
            for k in range(BLEND_GROUP):
                block = g * BLEND_GROUP + k
                at = pl.ds(pl.multiple_of(c + block * tile, tile), tile)
                slot = index_ref[at_row_last + c // tile + block]
                value = (
                    0.5 * (old[band, at] + land[band, at]) - LEARN_RATE * item_sum[slot, band]
                )
                out[band, at] = value
                if tiles is not None:
                    tiles[c // tile + block, band] = value
            return carry

        lax.fori_loop(0, width // tile // BLEND_GROUP, body, 0)

    groups = slots // GROUP
    stride = groups // pieces

    def first_grads(j, carry):
        grads(j * stride, (j + 1) * stride)
        return carry

    tiled(x, x_tiles)
    tiled(y, y_tiles)
    lax.fori_loop(0, pieces, first_grads, 0)
    collect()
    swap = to_partner(grad, grad_land, 1)
    swap.start()
    for j in range(pieces):
        forward(0, j)
        waiter(0, j).wait_recv()
        blend(x, land_a, x1, j, x_tiles)
        send(1, j)
        if j >= 1:
            forward(1, j - 1)
    forward(1, pieces - 1)
    swap.wait()
    y[...] = y[...] - LEARN_RATE * (grad[...] + grad_land[...])
    tiled(y, y_tiles)
    grads(0, groups)
    collect()
    other = pl.ds(pl.multiple_of((1 - item) * own, own), own)
    swap = to_partner(grad.at[:, other], part_land, 2)
    swap.start()
    for j in range(pieces):
        waiter(1, j).wait_recv()
        blend(x1, land_b, x_out, j)
    swap.wait()
    y_out[...] = y[:, mine] - LEARN_RATE * (grad[:, mine] + part_land[...])
    for j in range(pieces):
        for flow in range(2):
            waiter(flow, j).wait_send()
            forwarded(flow, j)


def two_steps_fused(hops, item_here, user_here, slot_values, row_index, column_index, block_total):
    rank, items = item_here.shape
    slots, tile = slot_values.shape[0], slot_values.shape[-1]
    own = user_here.shape[1]
    users = own * lax.axis_size("item")
    index = slot_index(row_index, column_index, items // tile, users // tile)
    live = (jnp.arange(slots, dtype=jnp.int32) < block_total[0]).astype(jnp.float32)
    scalars = pl.BlockSpec(memory_space=pltpu.SMEM)
    whole = pl.BlockSpec(memory_space=pltpu.VMEM)
    anywhere = pl.BlockSpec(memory_space=pl.ANY)
    held = lambda *shape: pltpu.VMEM(shape, jnp.float32)
    relay = held(PIECES, rank * HALVES // PIECES, items // (HALVES * RELAYS))
    return pl.pallas_call(
        partial(fused_kernel, hops),
        out_shape=[
            jax.ShapeDtypeStruct((rank, items), jnp.float32),
            jax.ShapeDtypeStruct((rank, own), jnp.float32),
        ],
        in_specs=[scalars, scalars, anywhere, anywhere, anywhere],
        out_specs=[whole, whole],
        scratch_shapes=[held(rank, items)] * 4
        + [relay, relay]
        + [pltpu.VMEM(slot_values.shape, slot_values.dtype)]
        + [held(slots + 1, rank, tile)] * 2
        + [held(rank, users)] * 3
        + [held(rank, own), held(items // tile, rank, tile), held(users // tile, rank, tile)]
        + [pltpu.SemaphoreType.DMA((PIECES,))] * 8
        + [pltpu.SemaphoreType.DMA((6,)), pltpu.SemaphoreType.DMA((3,))],
        compiler_params=pltpu.CompilerParams(
            collective_id=1 + hops[0], has_side_effects=True, vmem_limit_bytes=48 << 20
        ),
        cost_estimate=pl.CostEstimate(
            flops=20 * slots * tile * tile * rank,
            bytes_accessed=16 * rank * items,
            transcendentals=0,
        ),
    )(index, live, item_here, user_here, slot_values)


def per_device(item_factors, user_factors, ratings, block_rows, block_cols, block_count, hop_steps):
    mixed = lambda pair: (
        1 not in pair
        and lax.axis_size("item") == 2
        and lax.axis_size("site") % RELAYS == 0
        and lax.axis_size("site") > 2 * RELAYS
    )
    pairs = [(a, b) for a in range(HOPS) for b in range(HOPS) if a != b]
    first, second = hop_steps[0], hop_steps[1]
    chosen = first * (HOPS - 1) + second - (second > first).astype(jnp.int32)
    item_here, user_here = lax.switch(
        chosen,
        [partial(two_steps_fused if mixed(pair) else two_steps, pair) for pair in pairs],
        item_factors[0],
        user_factors[0],
        ratings[0, 0],
        block_rows[0, 0],
        block_cols[0, 0],
        block_count[0],
    )
    return (item_here[None], user_here[None])


def solution(mesh):
    return jax.shard_map(
        per_device,
        mesh=mesh,
        in_specs=(
            P("site", None, "item"),
            P("site", None, "item"),
            P("site", "item", None, None, None),
            P("site", "item", None),
            P("site", "item", None),
            P("site", "item"),
            P(),
        ),
        out_specs=(P("site", None, "item"), P("site", None, "item")),
        check_vma=False,
    )
```

```python
from functools import partial

import jax
import jax.numpy as jnp
from jax import lax
from jax.experimental import pallas as pl
from jax.experimental.pallas import tpu as pltpu
from jax.sharding import PartitionSpec as P

ITERS = 2
HOPS = 3
LEARN_RATE = 0.05
CHUNKS = 4
GROUP = 8
RELAYS = 4
KERNEL_WEIGHT = 450
PIECES = 8
FUSED_GROUP = 16
WINDOW = 2
LEAD = 2
LOOK = 1
SIDE = 1
EARLY = 4
HALVES = 2
BLEND_GROUP = 8
BLEND_STEPS = 8


def passed_along(block, axis, distance):
    devices = range(lax.axis_size(axis))
    route = [((i - distance) % len(devices), i) for i in devices]
    return lax.ppermute(block, axis, route)


def split_high_low(values):
    high = values.astype(jnp.bfloat16)
    low = (values - high.astype(jnp.float32)).astype(jnp.bfloat16)
    return high, low


def dot_f32(lhs, rhs, lhs_dim, rhs_dim):
    return lax.dot_general(
        lhs, rhs, (((lhs_dim,), (rhs_dim,)), ((), ())), preferred_element_type=jnp.float32
    )


def grads_kernel(chunks, rows_ref, cols_ref, count_ref, *refs):
    x_refs = refs[:chunks]
    y_ref, ratings_ref = refs[chunks : chunks + 2]
    base_ref, user_ref = refs[chunks + 2 :]
    group, tile = ratings_ref.shape[0], ratings_ref.shape[-1]
    rank = y_ref.shape[0]
    first = pl.program_id(0) * group
    total = count_ref[0]

    @pl.when(pl.program_id(0) == 0)
    def _():
        start = 0
        for x_ref in x_refs:
            base_ref[start : start + x_ref.shape[0], :] = 0.5 * x_ref[...]
            start += x_ref.shape[0]
        user_ref[...] = jnp.zeros_like(user_ref)

    @pl.when(first < total)
    def _():
        parts = []
        for k in range(group):
            row = pl.ds(pl.multiple_of(rows_ref[first + k] * tile, tile), tile)
            col = pl.ds(pl.multiple_of(cols_ref[first + k] * tile, tile), tile)
            limit = jnp.where(first + k < total, 1.0, 0.0).astype(jnp.float32)
            x = jnp.concatenate([x_ref[:, row] for x_ref in x_refs], axis=0)
            x_high, x_low = split_high_low(x)
            y_high, y_low = split_high_low(y_ref[:, col])
            rebuilt = dot_f32(
                jnp.concatenate([x_high, x_low, x_high], axis=0),
                jnp.concatenate([y_high, y_high, y_low], axis=0),
                0,
                0,
            )
            clipped = jnp.clip(rebuilt - ratings_ref[k].astype(jnp.float32), -limit, limit)
            c_high, c_low = split_high_low(clipped)
            item_pair = dot_f32(jnp.concatenate([y_high, y_low], axis=0), c_high, 1, 1)
            item_part = item_pair[:rank] + item_pair[rank:] + dot_f32(y_high, c_low, 1, 1)
            user_pair = dot_f32(jnp.concatenate([x_high, x_low], axis=0), c_high, 1, 0)
            user_part = user_pair[:rank] + user_pair[rank:] + dot_f32(x_high, c_low, 1, 0)
            parts.append((row, col, item_part, user_part))
        for row, col, item_part, user_part in parts:
            base_ref[:, row] -= LEARN_RATE * item_part
            user_ref[:, col] += user_part


def local_grads(x_parts, users_whole, slot_values, row_index, column_index, block_total):
    chunks = len(x_parts)
    slot_total, tile = slot_values.shape[0], slot_values.shape[-1]
    rank, users = users_whole.shape
    items = x_parts[0].shape[1]
    once = pl.Buffered(1)
    held = lambda shape: pl.BlockSpec(shape, lambda i, *_: (0, 0), pipeline_mode=once)
    return pl.pallas_call(
        partial(grads_kernel, chunks),
        grid_spec=pltpu.PrefetchScalarGridSpec(
            num_scalar_prefetch=3,
            grid=(slot_total // GROUP,),
            in_specs=[held(part.shape) for part in x_parts]
            + [held((rank, users)), pl.BlockSpec((GROUP, tile, tile), lambda i, *_: (i, 0, 0))],
            out_specs=[held((rank, items)), held((rank, users))],
        ),
        out_shape=[
            jax.ShapeDtypeStruct((rank, items), jnp.float32),
            jax.ShapeDtypeStruct((rank, users), jnp.float32),
        ],
        compiler_params=pltpu.CompilerParams(vmem_limit_bytes=24 << 20),
        cost_estimate=pl.CostEstimate(
            flops=KERNEL_WEIGHT * slot_total * tile * tile * rank,
            bytes_accessed=8 * rank * items + 2 * slot_total * tile * tile,
            transcendentals=0,
        ),
    )(row_index, column_index, block_total, *x_parts, users_whole, slot_values)


def over_items(block):
    total = block
    for distance in range(1, lax.axis_size("item")):
        total = total + passed_along(block, "item", distance)
    return total


def owned_part(whole):
    count = lax.axis_size("item")
    width = whole.shape[1] // count
    me = lax.axis_index("item")
    cut = lambda who: lax.dynamic_slice_in_dim(whole, who * width, width, axis=1)
    total = cut(me)
    for distance in range(1, count):
        total = total + passed_along(cut(lax.rem(me + distance, count)), "item", distance)
    return total


def kept_part(whole):
    width = whole.shape[1] // lax.axis_size("item")
    return lax.dynamic_slice_in_dim(whole, lax.axis_index("item") * width, width, axis=1)


def blend_kernel(base_ref, *refs):
    out_ref = refs[-1]
    start = 0
    for ref in refs[:-1]:
        rows = slice(start, start + ref.shape[0])
        out_ref[rows, :] = base_ref[rows, :] + 0.5 * ref[...]
        start += ref.shape[0]


def blend(base, peers):
    rank, items = base.shape
    width = items // BLEND_STEPS
    spec = lambda rows: pl.BlockSpec((rows, width), lambda i: (0, i))
    return pl.pallas_call(
        blend_kernel,
        grid=(BLEND_STEPS,),
        in_specs=[spec(rank)] + [spec(peer.shape[0]) for peer in peers],
        out_specs=spec(rank),
        out_shape=jax.ShapeDtypeStruct((rank, items), jnp.float32),
    )(base, *peers)


def cut_rows(block):
    size = block.shape[0] // CHUNKS
    return [block[c * size : (c + 1) * size] for c in range(CHUNKS)]


def two_steps(hops, item_here, user_here, slot_values, row_index, column_index, block_total):
    grads = lambda parts, users: local_grads(
        parts, users, slot_values, row_index, column_index, block_total
    )
    peers = [passed_along(part, "site", -(1 << hops[0])) for part in cut_rows(item_here)]
    users_whole = lax.all_gather(user_here, "item", axis=1, tiled=True)
    base, user_grad = grads([item_here], users_whole)
    users_whole = users_whole - LEARN_RATE * over_items(user_grad)
    x_parts = [part + 0.5 * peer for part, peer in zip(cut_rows(base), peers)]
    peers = [passed_along(part, "site", -(1 << hops[1])) for part in x_parts]
    base, user_grad = grads(x_parts, users_whole)
    return blend(base, peers), kept_part(users_whole) - LEARN_RATE * owned_part(user_grad)


def strongest(values):
    while values.shape[0] > 1:
        half = values.shape[0] // 2
        values = jnp.maximum(values[:half], values[half:])
    return values


def slot_links(keys, blocks):
    slots = keys.shape[1]
    here = jnp.broadcast_to(keys, (slots, slots))
    there = here.T
    slot = lax.broadcasted_iota(jnp.int32, (slots, slots), 0)
    lane = lax.broadcasted_iota(jnp.int32, (slots, slots), 1)

    def latest(hit):
        found = strongest(jnp.where(hit, slot, -1))
        return jnp.where(found < 0, slots, found)

    before = latest(jnp.logical_and(there == here, slot < lane))
    return [before] + [latest(there == lane + start) for start in range(0, blocks, slots)]


def fused_kernel(hops, count_ref, rows_in, cols_in, x_in, y_in, ratings_in, x_out, y_out, *refs):
    x, x1, land_a, land_b, relay_a, relay_b, ratings, item_sum, user_sum = refs[:9]
    y, grad, grad_land, part_land, x_tiles, y_tiles = refs[9:15]
    links, index = refs[15:17]
    send_a, recv_a, send_b, recv_b, take_a, give_a, take_b, give_b, swaps, loads = refs[17:]
    site, item = lax.axis_index("site"), lax.axis_index("item")
    sites = lax.axis_size("site")
    place = lax.rem(site, RELAYS)
    layer = site - place
    last = RELAYS - 1
    ahead = lax.rem(site + sites - RELAYS, sites)
    behind = lax.rem(site + RELAYS, sites)
    ahead_layer, behind_layer = ahead - place, behind - place
    rank, items = x.shape
    own = y_in.shape[1]
    users = y.shape[1]
    slots, tile = ratings.shape[0], ratings.shape[-1]
    row_blocks, column_blocks = items // tile, users // tile
    pieces = PIECES
    rows = rank // (pieces // HALVES)
    width = items // HALVES
    part = width // RELAYS
    at_row_last = 3
    at_col_prev = at_row_last + -(-row_blocks // slots)
    at_col_last = at_col_prev + 1

    def spot(j):
        return (j // HALVES) * rows, (j % HALVES) * width

    def view(ref, j):
        r, c = spot(j)
        return ref.at[pl.ds(r, rows), pl.ds(c, width)]

    def slab(ref, j, q, count=1):
        r, c = spot(j)
        return ref.at[pl.ds(r, rows), pl.ds(c + q * part, count * part)]

    def copy(src, dst, send, recv, target):
        return pltpu.make_async_remote_copy(
            src_ref=src,
            dst_ref=dst,
            send_sem=send,
            recv_sem=recv,
            device_id=(item, target),
            device_id_type=pl.DeviceIdType.MESH,
        )

    def to_partner(src, dst, k):
        return pltpu.make_async_remote_copy(
            src_ref=src,
            dst_ref=dst,
            send_sem=swaps.at[2 * k],
            recv_sem=swaps.at[2 * k + 1],
            device_id=(1 - item, site),
            device_id_type=pl.DeviceIdType.MESH,
        )

    flows = (
        (hops[0], x_in, land_a, relay_a, send_a, recv_a, take_a, give_a),
        (hops[1], x1, land_b, relay_b, send_b, recv_b, take_b, give_b),
    )

    def send(flow, j):
        hop, src, land, relay, send_sem, recv_sem, take, give = flows[flow]
        if hop != 0:
            copy(view(src, j), view(land, j), send_sem.at[j], recv_sem.at[j], ahead).start()
            return
        for here in range(1, RELAYS):

            @pl.when(place == here)
            def _():
                count = last if here == 2 else RELAYS
                copy(
                    slab(src, j, 0, count),
                    slab(land, j, 0, count),
                    send_sem.at[j],
                    recv_sem.at[j],
                    site - 1,
                ).start()
                if here == 2:
                    copy(
                        slab(src, j, last), relay.at[j], send_sem.at[j], take.at[j], site - 2
                    ).start()

        @pl.when(place == 0)
        def _():
            for q in range(last, 0, -1):
                copy(slab(src, j, q), relay.at[j], send_sem.at[j], take.at[j], site + q).start()
            if flow == 0:
                climb(flow, j)

    def climb(flow, j):
        hop, src, land, relay, send_sem, recv_sem, take, give = flows[flow]
        copy(
            slab(src, j, 0), slab(land, j, 0), send_sem.at[j], recv_sem.at[j], ahead + last
        ).start()

    def forward(flow, j, here):
        hop, src, land, relay, send_sem, recv_sem, take, give = flows[flow]
        if hop != 0:
            return

        @pl.when(place == here)
        def _():
            q, target = (last, layer + 1) if here == 0 else (here, ahead_layer + last)
            copy(relay.at[j], relay.at[j], give.at[j], take.at[j], ahead).wait_recv()
            copy(relay.at[j], slab(land, j, q), give.at[j], recv_sem.at[j], target).start()

    def ascend(flow, j):
        for here in range(1, RELAYS):
            forward(flow, j, here)

    def forwarded(flow, j):
        hop, src, land, relay, send_sem, recv_sem, take, give = flows[flow]
        if hop != 0:
            return

        copy(relay.at[j], relay.at[j], give.at[j], take.at[j], ahead).wait_send()

    def waiter(flow, j):
        hop, src, land, relay, send_sem, recv_sem, take, give = flows[flow]
        return copy(view(src, j), view(land, j), send_sem.at[j], recv_sem.at[j], ahead)

    barrier = pltpu.get_barrier_semaphore()

    def greet(core, peer):
        pl.semaphore_signal(
            barrier, inc=1, device_id=(core, peer), device_id_type=pl.DeviceIdType.MESH
        )

    for k in range(1, RELAYS):
        greet(item, layer + lax.rem(place + k, RELAYS))
    greet(item, ahead)
    greet(item, behind)
    greet(1 - item, site)

    @pl.when(place != last)
    def _():
        greet(item, ahead_layer + last)
        pl.semaphore_wait(barrier, RELAYS + 3)

    @pl.when(place == last)
    def _():
        for q in range(last):
            greet(item, behind_layer + q)
        pl.semaphore_wait(barrier, RELAYS + 2 + last)

    mine = pl.ds(pl.multiple_of(item * own, own), own)
    swap = to_partner(y_in, y.at[:, mine], 0)
    swap.start()
    low = hops[0] == 0
    window = min(WINDOW, pieces)
    wide = min(LEAD, pieces) if low else window
    for j in range(window):
        send(0, j)
    if wide > window:

        @pl.when(place == 0)
        def _():
            for j in range(window, wide):
                send(0, j)

    take_x = pltpu.make_async_copy(x_in, x, loads.at[0])
    take_y = pltpu.make_async_copy(y_in, y.at[:, mine], loads.at[1])
    take_ratings = pltpu.make_async_copy(ratings_in, ratings, loads.at[2])
    take_x.start()
    take_y.start()
    take_ratings.start()
    row_links = slot_links(rows_in[...], row_blocks)
    col_links = slot_links(cols_in[...], column_blocks)
    lines = [rows_in[...], cols_in[...]] + row_links + col_links
    for at, line in enumerate(lines):
        links[at : at + 1, :] = line
    take_index = pltpu.make_async_copy(links, index, loads.at[3])
    take_index.start()
    item_sum[slots] = jnp.zeros((rank, tile), jnp.float32)
    user_sum[slots] = jnp.zeros((rank, tile), jnp.float32)
    take_index.wait()
    take_x.wait()
    take_y.wait()
    swap.wait()
    take_ratings.wait()

    def tiled(src, dst):
        def body(c, carry):
            dst[c] = src[:, pl.ds(pl.multiple_of(c * tile, tile), tile)]
            return carry

        lax.fori_loop(0, dst.shape[0], body, 0, unroll=8)

    total = count_ref[0]

    def grad_group(first):
        parts = []
        for k in range(FUSED_GROUP):
            slot = first + k
            limit = jnp.clip(total - slot, 0, 1).astype(jnp.float32)
            x_high, x_low = split_high_low(x_tiles[index[0, slot]])
            y_high, y_low = split_high_low(y_tiles[index[1, slot]])
            rebuilt = dot_f32(
                jnp.concatenate([x_high, x_low, x_high], axis=0),
                jnp.concatenate([y_high, y_high, y_low], axis=0),
                0,
                0,
            )
            clipped = jnp.clip(rebuilt - ratings[slot].astype(jnp.float32), -limit, limit)
            c_high, c_low = split_high_low(clipped)
            item_part = dot_f32(
                jnp.concatenate([y_high, y_low, y_high], axis=1),
                jnp.concatenate([c_high, c_high, c_low], axis=1),
                1,
                1,
            )
            user_part = dot_f32(
                jnp.concatenate([x_high, x_low, x_high], axis=1),
                jnp.concatenate([c_high, c_high, c_low], axis=0),
                1,
                0,
            )
            parts.append((slot, item_part, user_part))
        for slot, item_part, user_part in parts:
            item_sum[slot] = item_part + item_sum[index[2, slot]]
            user_sum[slot] = user_part + user_sum[index[at_col_prev, slot]]

    def grads(start, stop):
        def body(g, carry):
            grad_group(g * FUSED_GROUP)
            return carry

        lax.fori_loop(start, stop, body, 0)

    def collect():
        def body(c, carry):
            at = pl.ds(pl.multiple_of(c * tile, tile), tile)
            grad[:, at] = user_sum[index[at_col_last, c]]
            return carry

        lax.fori_loop(0, column_blocks, body, 0)

    def blend(old, land, out, j, tiles=None):
        r, c = spot(j)
        band = slice(r, r + rows)
        line, lane = at_row_last + c // tile // slots, c // tile % slots

        def body(g, carry):
            for k in range(BLEND_GROUP):
                block = g * BLEND_GROUP + k
                at = pl.ds(pl.multiple_of(c + block * tile, tile), tile)
                slot = index[line, lane + block]
                value = (
                    0.5 * (old[band, at] + land[band, at]) - LEARN_RATE * item_sum[slot, band]
                )
                out[band, at] = value
                if tiles is not None:
                    tiles[c // tile + block, band] = value
            return carry

        lax.fori_loop(0, width // tile // BLEND_GROUP, body, 0)

    groups = slots // FUSED_GROUP

    def pace(j, limit):
        waiter(0, j).wait_send()
        if j + limit < pieces:
            send(0, j + limit)

    def sent(j):
        if wide == window:
            pace(j, window)
            return

        @pl.when(place == 0)
        def _():
            pace(j, wide)

        @pl.when(place != 0)
        def _():
            pace(j, window)

    def rise(j):
        if hops[1] != 0:
            return

        @pl.when(place == 0)
        def _():
            climb(1, j)

        ascend(1, j)

    tiled(x, x_tiles)
    tiled(y, y_tiles)
    grads(0, groups)
    collect()
    swap = to_partner(grad, grad_land, 1)
    swap.start()
    for j in range(pieces):
        for k in range(j + SIDE if j else 0, min(j + SIDE + 1, pieces)):
            forward(0, k, 0)
        for k in range(j + LOOK if j else 0, min(j + LOOK + 1, pieces)):
            ascend(0, k)
        waiter(0, j).wait_recv()
        sent(j)
        blend(x, land_a, x1, j, x_tiles)
        send(1, j)
        if j >= 1:
            forward(1, j - 1, 0)
            if j <= EARLY:
                rise(j - 1)
    forward(1, pieces - 1, 0)
    for j in range(min(EARLY, pieces - 1), pieces):
        rise(j)
    swap.wait()
    y[...] = y[...] - LEARN_RATE * (grad[...] + grad_land[...])
    tiled(y, y_tiles)
    grads(0, groups)
    collect()
    other = pl.ds(pl.multiple_of((1 - item) * own, own), own)
    swap = to_partner(grad.at[:, other], part_land, 2)
    swap.start()
    for j in range(pieces):
        waiter(1, j).wait_recv()
        blend(x1, land_b, x_out, j)
    swap.wait()
    y_out[...] = y[:, mine] - LEARN_RATE * (grad[:, mine] + part_land[...])
    for j in range(pieces):
        waiter(1, j).wait_send()
        for flow in range(2):
            forwarded(flow, j)


def handed_over(*blocks):
    count = len(blocks)

    def kernel(*refs):
        sems = refs[-1]
        copies = [
            pltpu.make_async_copy(refs[k], refs[count + k], sems.at[k]) for k in range(count)
        ]
        for copy in copies:
            copy.start()
        for copy in copies:
            copy.wait()

    return pl.pallas_call(
        kernel,
        out_shape=[jax.ShapeDtypeStruct(block.shape, block.dtype) for block in blocks],
        in_specs=[pl.BlockSpec(memory_space=pltpu.VMEM)] * count,
        out_specs=[pl.BlockSpec(memory_space=pl.ANY)] * count,
        scratch_shapes=[pltpu.SemaphoreType.DMA((count,))],
        compiler_params=pltpu.CompilerParams(vmem_limit_bytes=8 << 20),
    )(*blocks)


def two_steps_fused(hops, item_here, user_here, slot_values, row_index, column_index, block_total):
    rank, items = item_here.shape
    slots, tile = slot_values.shape[0], slot_values.shape[-1]
    own = user_here.shape[1]
    users = own * lax.axis_size("item")
    lines = 4 + -(-items // (tile * slots)) + -(-users // (tile * slots))
    lines = -(-lines // 8) * 8
    scalars = pl.BlockSpec(memory_space=pltpu.SMEM)
    whole = pl.BlockSpec(memory_space=pltpu.VMEM)
    anywhere = pl.BlockSpec(memory_space=pl.ANY)
    held = lambda *shape: pltpu.VMEM(shape, jnp.float32)
    relay = held(PIECES, rank * HALVES // PIECES, items // (HALVES * RELAYS))
    mixed, kept = pl.pallas_call(
        partial(fused_kernel, hops),
        out_shape=[
            jax.ShapeDtypeStruct((rank, items), jnp.float32),
            jax.ShapeDtypeStruct((rank, own), jnp.float32),
        ],
        in_specs=[scalars, whole, whole, anywhere, anywhere, anywhere],
        out_specs=[whole, whole],
        scratch_shapes=[held(rank, items)] * 4
        + [relay, relay]
        + [pltpu.VMEM(slot_values.shape, slot_values.dtype)]
        + [held(slots + 1, rank, tile)] * 2
        + [held(rank, users)] * 3
        + [held(rank, own), held(items // tile, rank, tile), held(users // tile, rank, tile)]
        + [pltpu.VMEM((lines, slots), jnp.int32), pltpu.SMEM((lines, slots), jnp.int32)]
        + [pltpu.SemaphoreType.DMA((PIECES,))] * 8
        + [pltpu.SemaphoreType.DMA((6,)), pltpu.SemaphoreType.DMA((4,))],
        compiler_params=pltpu.CompilerParams(
            collective_id=1 + hops[0], has_side_effects=True, vmem_limit_bytes=48 << 20
        ),
        cost_estimate=pl.CostEstimate(
            flops=20 * slots * tile * tile * rank,
            bytes_accessed=16 * rank * items,
            transcendentals=0,
        ),
    )(block_total, row_index[None], column_index[None], item_here, user_here, slot_values)
    return handed_over(mixed, kept)


def per_device(item_factors, user_factors, ratings, block_rows, block_cols, block_count, hop_steps):
    mixed = lambda pair: (
        1 not in pair
        and lax.axis_size("item") == 2
        and lax.axis_size("site") % RELAYS == 0
        and lax.axis_size("site") > 2 * RELAYS
    )
    pairs = [(a, b) for a in range(HOPS) for b in range(HOPS) if a != b]
    first, second = hop_steps[0], hop_steps[1]
    chosen = first * (HOPS - 1) + second - (second > first).astype(jnp.int32)
    item_here, user_here = lax.switch(
        chosen,
        [partial(two_steps_fused if mixed(pair) else two_steps, pair) for pair in pairs],
        item_factors[0],
        user_factors[0],
        ratings[0, 0],
        block_rows[0, 0],
        block_cols[0, 0],
        block_count[0],
    )
    return (item_here[None], user_here[None])


def solution(mesh):
    return jax.shard_map(
        per_device,
        mesh=mesh,
        in_specs=(
            P("site", None, "item"),
            P("site", None, "item"),
            P("site", "item", None, None, None),
            P("site", "item", None),
            P("site", "item", None),
            P("site", "item"),
            P(),
        ),
        out_specs=(P("site", None, "item"), P("site", None, "item")),
        check_vma=False,
    )
```

```python
from functools import partial

import jax
import jax.numpy as jnp
from jax import lax
from jax.experimental import pallas as pl
from jax.experimental.pallas import tpu as pltpu
from jax.sharding import PartitionSpec as P

ITERS = 2
HOPS = 3
LEARN_RATE = 0.05
CHUNKS = 4
GROUP = 8
RELAYS = 4
KERNEL_WEIGHT = 450
PIECES = 16
FUSED_GROUP = 16
WINDOW = 3
LEAD = 3
LOOK = 2
SIDE = 2
EARLY = 12
BLEND_GROUP = 8
BLEND_STEPS = 8


def passed_along(block, axis, distance):
    devices = range(lax.axis_size(axis))
    route = [((i - distance) % len(devices), i) for i in devices]
    return lax.ppermute(block, axis, route)


def split_high_low(values):
    high = values.astype(jnp.bfloat16)
    low = (values - high.astype(jnp.float32)).astype(jnp.bfloat16)
    return high, low


def dot_f32(lhs, rhs, lhs_dim, rhs_dim):
    return lax.dot_general(
        lhs, rhs, (((lhs_dim,), (rhs_dim,)), ((), ())), preferred_element_type=jnp.float32
    )


def grads_kernel(chunks, rows_ref, cols_ref, count_ref, *refs):
    x_refs = refs[:chunks]
    y_ref, ratings_ref = refs[chunks : chunks + 2]
    base_ref, user_ref = refs[chunks + 2 :]
    group, tile = ratings_ref.shape[0], ratings_ref.shape[-1]
    rank = y_ref.shape[0]
    first = pl.program_id(0) * group
    total = count_ref[0]

    @pl.when(pl.program_id(0) == 0)
    def _():
        start = 0
        for x_ref in x_refs:
            base_ref[start : start + x_ref.shape[0], :] = 0.5 * x_ref[...]
            start += x_ref.shape[0]
        user_ref[...] = jnp.zeros_like(user_ref)

    @pl.when(first < total)
    def _():
        parts = []
        for k in range(group):
            row = pl.ds(pl.multiple_of(rows_ref[first + k] * tile, tile), tile)
            col = pl.ds(pl.multiple_of(cols_ref[first + k] * tile, tile), tile)
            limit = jnp.where(first + k < total, 1.0, 0.0).astype(jnp.float32)
            x = jnp.concatenate([x_ref[:, row] for x_ref in x_refs], axis=0)
            x_high, x_low = split_high_low(x)
            y_high, y_low = split_high_low(y_ref[:, col])
            rebuilt = dot_f32(
                jnp.concatenate([x_high, x_low, x_high], axis=0),
                jnp.concatenate([y_high, y_high, y_low], axis=0),
                0,
                0,
            )
            clipped = jnp.clip(rebuilt - ratings_ref[k].astype(jnp.float32), -limit, limit)
            c_high, c_low = split_high_low(clipped)
            item_pair = dot_f32(jnp.concatenate([y_high, y_low], axis=0), c_high, 1, 1)
            item_part = item_pair[:rank] + item_pair[rank:] + dot_f32(y_high, c_low, 1, 1)
            user_pair = dot_f32(jnp.concatenate([x_high, x_low], axis=0), c_high, 1, 0)
            user_part = user_pair[:rank] + user_pair[rank:] + dot_f32(x_high, c_low, 1, 0)
            parts.append((row, col, item_part, user_part))
        for row, col, item_part, user_part in parts:
            base_ref[:, row] -= LEARN_RATE * item_part
            user_ref[:, col] += user_part


def local_grads(x_parts, users_whole, slot_values, row_index, column_index, block_total):
    chunks = len(x_parts)
    slot_total, tile = slot_values.shape[0], slot_values.shape[-1]
    rank, users = users_whole.shape
    items = x_parts[0].shape[1]
    once = pl.Buffered(1)
    held = lambda shape: pl.BlockSpec(shape, lambda i, *_: (0, 0), pipeline_mode=once)
    return pl.pallas_call(
        partial(grads_kernel, chunks),
        grid_spec=pltpu.PrefetchScalarGridSpec(
            num_scalar_prefetch=3,
            grid=(slot_total // GROUP,),
            in_specs=[held(part.shape) for part in x_parts]
            + [held((rank, users)), pl.BlockSpec((GROUP, tile, tile), lambda i, *_: (i, 0, 0))],
            out_specs=[held((rank, items)), held((rank, users))],
        ),
        out_shape=[
            jax.ShapeDtypeStruct((rank, items), jnp.float32),
            jax.ShapeDtypeStruct((rank, users), jnp.float32),
        ],
        compiler_params=pltpu.CompilerParams(vmem_limit_bytes=24 << 20),
        cost_estimate=pl.CostEstimate(
            flops=KERNEL_WEIGHT * slot_total * tile * tile * rank,
            bytes_accessed=8 * rank * items + 2 * slot_total * tile * tile,
            transcendentals=0,
        ),
    )(row_index, column_index, block_total, *x_parts, users_whole, slot_values)


def over_items(block):
    total = block
    for distance in range(1, lax.axis_size("item")):
        total = total + passed_along(block, "item", distance)
    return total


def owned_part(whole):
    count = lax.axis_size("item")
    width = whole.shape[1] // count
    me = lax.axis_index("item")
    cut = lambda who: lax.dynamic_slice_in_dim(whole, who * width, width, axis=1)
    total = cut(me)
    for distance in range(1, count):
        total = total + passed_along(cut(lax.rem(me + distance, count)), "item", distance)
    return total


def kept_part(whole):
    width = whole.shape[1] // lax.axis_size("item")
    return lax.dynamic_slice_in_dim(whole, lax.axis_index("item") * width, width, axis=1)


def blend_kernel(base_ref, *refs):
    out_ref = refs[-1]
    start = 0
    for ref in refs[:-1]:
        rows = slice(start, start + ref.shape[0])
        out_ref[rows, :] = base_ref[rows, :] + 0.5 * ref[...]
        start += ref.shape[0]


def blend(base, peers):
    rank, items = base.shape
    width = items // BLEND_STEPS
    spec = lambda rows: pl.BlockSpec((rows, width), lambda i: (0, i))
    return pl.pallas_call(
        blend_kernel,
        grid=(BLEND_STEPS,),
        in_specs=[spec(rank)] + [spec(peer.shape[0]) for peer in peers],
        out_specs=spec(rank),
        out_shape=jax.ShapeDtypeStruct((rank, items), jnp.float32),
    )(base, *peers)


def cut_rows(block):
    size = block.shape[0] // CHUNKS
    return [block[c * size : (c + 1) * size] for c in range(CHUNKS)]


def two_steps(hops, item_here, user_here, slot_values, row_index, column_index, block_total):
    grads = lambda parts, users: local_grads(
        parts, users, slot_values, row_index, column_index, block_total
    )
    peers = [passed_along(part, "site", -(1 << hops[0])) for part in cut_rows(item_here)]
    users_whole = lax.all_gather(user_here, "item", axis=1, tiled=True)
    base, user_grad = grads([item_here], users_whole)
    users_whole = users_whole - LEARN_RATE * over_items(user_grad)
    x_parts = [part + 0.5 * peer for part, peer in zip(cut_rows(base), peers)]
    peers = [passed_along(part, "site", -(1 << hops[1])) for part in x_parts]
    base, user_grad = grads(x_parts, users_whole)
    return blend(base, peers), kept_part(users_whole) - LEARN_RATE * owned_part(user_grad)


def strongest(values):
    while values.shape[0] > 1:
        half = values.shape[0] // 2
        values = jnp.maximum(values[:half], values[half:])
    return values


def slot_links(keys, blocks):
    slots = keys.shape[1]
    here = jnp.broadcast_to(keys, (slots, slots))
    there = here.T
    slot = lax.broadcasted_iota(jnp.int32, (slots, slots), 0)
    lane = lax.broadcasted_iota(jnp.int32, (slots, slots), 1)

    def latest(hit):
        found = strongest(jnp.where(hit, slot, -1))
        return jnp.where(found < 0, slots, found)

    before = latest(jnp.logical_and(there == here, slot < lane))
    return [before] + [latest(there == lane + start) for start in range(0, blocks, slots)]


def fused_kernel(hops, count_ref, rows_in, cols_in, x_in, y_in, ratings_in, x_out, y_out, *refs):
    x, x1, land_a, land_b, relay_a, relay_b, ratings, item_sum, user_sum = refs[:9]
    y, grad, grad_land, part_land, x_tiles, y_tiles = refs[9:15]
    links, index = refs[15:17]
    send_a, recv_a, send_b, recv_b, take_a, give_a, take_b, give_b, swaps, loads = refs[17:]
    site, item = lax.axis_index("site"), lax.axis_index("item")
    sites = lax.axis_size("site")
    place = lax.rem(site, RELAYS)
    layer = site - place
    last = RELAYS - 1
    ahead = lax.rem(site + sites - RELAYS, sites)
    behind = lax.rem(site + RELAYS, sites)
    ahead_layer, behind_layer = ahead - place, behind - place
    rank, items = x.shape
    own = y_in.shape[1]
    users = y.shape[1]
    slots, tile = ratings.shape[0], ratings.shape[-1]
    row_blocks, column_blocks = items // tile, users // tile
    pieces = PIECES
    width = items // pieces
    part = width // RELAYS
    at_row_last = 3
    at_col_prev = at_row_last + -(-row_blocks // slots)
    at_col_last = at_col_prev + 1

    def view(ref, j):
        return ref.at[:, pl.ds(pl.multiple_of(j * width, tile), width)]

    def slab(ref, j, q, count=1):
        return ref.at[:, pl.ds(pl.multiple_of(j * width + q * part, tile), count * part)]

    def copy(src, dst, send, recv, target):
        return pltpu.make_async_remote_copy(
            src_ref=src,
            dst_ref=dst,
            send_sem=send,
            recv_sem=recv,
            device_id=(item, target),
            device_id_type=pl.DeviceIdType.MESH,
        )

    def to_partner(src, dst, k):
        return pltpu.make_async_remote_copy(
            src_ref=src,
            dst_ref=dst,
            send_sem=swaps.at[2 * k],
            recv_sem=swaps.at[2 * k + 1],
            device_id=(1 - item, site),
            device_id_type=pl.DeviceIdType.MESH,
        )

    flows = (
        (hops[0], x_in, land_a, relay_a, send_a, recv_a, take_a, give_a),
        (hops[1], x1, land_b, relay_b, send_b, recv_b, take_b, give_b),
    )

    def send(flow, j):
        hop, src, land, relay, send_sem, recv_sem, take, give = flows[flow]
        if hop != 0:
            copy(view(src, j), view(land, j), send_sem.at[j], recv_sem.at[j], ahead).start()
            return
        for here in range(1, RELAYS):

            @pl.when(place == here)
            def _():
                count = last if here == 2 else RELAYS
                copy(
                    slab(src, j, 0, count),
                    slab(land, j, 0, count),
                    send_sem.at[j],
                    recv_sem.at[j],
                    site - 1,
                ).start()
                if here == 2:
                    copy(
                        slab(src, j, last), relay.at[j], send_sem.at[j], take.at[j], site - 2
                    ).start()

        @pl.when(place == 0)
        def _():
            for q in range(last, 0, -1):
                copy(slab(src, j, q), relay.at[j], send_sem.at[j], take.at[j], site + q).start()
            if flow == 0:
                climb(flow, j)

    def climb(flow, j):
        hop, src, land, relay, send_sem, recv_sem, take, give = flows[flow]
        copy(
            slab(src, j, 0), slab(land, j, 0), send_sem.at[j], recv_sem.at[j], ahead + last
        ).start()

    def forward(flow, j, here):
        hop, src, land, relay, send_sem, recv_sem, take, give = flows[flow]
        if hop != 0:
            return

        @pl.when(place == here)
        def _():
            q, target = (last, layer + 1) if here == 0 else (here, ahead_layer + last)
            copy(relay.at[j], relay.at[j], give.at[j], take.at[j], ahead).wait_recv()
            copy(relay.at[j], slab(land, j, q), give.at[j], recv_sem.at[j], target).start()

    def ascend(flow, j):
        for here in range(1, RELAYS):
            forward(flow, j, here)

    def forwarded(flow, j):
        hop, src, land, relay, send_sem, recv_sem, take, give = flows[flow]
        if hop != 0:
            return

        copy(relay.at[j], relay.at[j], give.at[j], take.at[j], ahead).wait_send()

    def waiter(flow, j):
        hop, src, land, relay, send_sem, recv_sem, take, give = flows[flow]
        return copy(view(src, j), view(land, j), send_sem.at[j], recv_sem.at[j], ahead)

    barrier = pltpu.get_barrier_semaphore()

    def greet(core, peer):
        pl.semaphore_signal(
            barrier, inc=1, device_id=(core, peer), device_id_type=pl.DeviceIdType.MESH
        )

    for k in range(1, RELAYS):
        greet(item, layer + lax.rem(place + k, RELAYS))
    greet(item, ahead)
    greet(item, behind)
    greet(1 - item, site)

    @pl.when(place != last)
    def _():
        greet(item, ahead_layer + last)
        pl.semaphore_wait(barrier, RELAYS + 3)

    @pl.when(place == last)
    def _():
        for q in range(last):
            greet(item, behind_layer + q)
        pl.semaphore_wait(barrier, RELAYS + 2 + last)

    mine = pl.ds(pl.multiple_of(item * own, own), own)
    swap = to_partner(y_in, y.at[:, mine], 0)
    swap.start()
    low = hops[0] == 0
    window = min(WINDOW, pieces)
    wide = min(LEAD, pieces) if low else window
    for j in range(window):
        send(0, j)
    if wide > window:

        @pl.when(place == 0)
        def _():
            for j in range(window, wide):
                send(0, j)

    take_x = pltpu.make_async_copy(x_in, x, loads.at[0])
    take_y = pltpu.make_async_copy(y_in, y.at[:, mine], loads.at[1])
    take_ratings = pltpu.make_async_copy(ratings_in, ratings, loads.at[2])
    take_x.start()
    take_y.start()
    take_ratings.start()
    row_links = slot_links(rows_in[...], row_blocks)
    col_links = slot_links(cols_in[...], column_blocks)
    lines = [rows_in[...], cols_in[...]] + row_links + col_links
    for at, line in enumerate(lines):
        links[at : at + 1, :] = line
    take_index = pltpu.make_async_copy(links, index, loads.at[3])
    take_index.start()
    item_sum[slots] = jnp.zeros((rank, tile), jnp.float32)
    user_sum[slots] = jnp.zeros((rank, tile), jnp.float32)
    def tiled(src, dst):
        def body(c, carry):
            dst[c] = src[:, pl.ds(pl.multiple_of(c * tile, tile), tile)]
            return carry

        lax.fori_loop(0, dst.shape[0], body, 0, unroll=8)

    total = count_ref[0]

    def grad_group(first):
        parts = []
        for k in range(FUSED_GROUP):
            slot = first + k
            limit = jnp.clip(total - slot, 0, 1).astype(jnp.float32)
            x_high, x_low = split_high_low(x_tiles[index[0, slot]])
            y_high, y_low = split_high_low(y_tiles[index[1, slot]])
            rebuilt = dot_f32(
                jnp.concatenate([x_high, x_low, x_high], axis=0),
                jnp.concatenate([y_high, y_high, y_low], axis=0),
                0,
                0,
            )
            clipped = jnp.clip(rebuilt - ratings[slot].astype(jnp.float32), -limit, limit)
            c_high, c_low = split_high_low(clipped)
            item_part = dot_f32(
                jnp.concatenate([y_high, y_low, y_high], axis=1),
                jnp.concatenate([c_high, c_high, c_low], axis=1),
                1,
                1,
            )
            user_part = dot_f32(
                jnp.concatenate([x_high, x_low, x_high], axis=1),
                jnp.concatenate([c_high, c_high, c_low], axis=0),
                1,
                0,
            )
            parts.append((slot, item_part, user_part))
        for slot, item_part, user_part in parts:
            item_sum[slot] = item_part + item_sum[index[2, slot]]
            user_sum[slot] = user_part + user_sum[index[at_col_prev, slot]]

    def grads(start, stop):
        def body(g, carry):
            grad_group(g * FUSED_GROUP)
            return carry

        lax.fori_loop(start, stop, body, 0)

    def collect():
        def body(c, carry):
            at = pl.ds(pl.multiple_of(c * tile, tile), tile)
            grad[:, at] = user_sum[index[at_col_last, c]]
            return carry

        lax.fori_loop(0, column_blocks, body, 0)

    def blend(old, land, out, j, tiles=None):
        start = j * width // tile
        line, lane = at_row_last + start // slots, start % slots

        def body(g, carry):
            for k in range(BLEND_GROUP):
                block = g * BLEND_GROUP + k
                at = pl.ds(pl.multiple_of((start + block) * tile, tile), tile)
                slot = index[line, lane + block]
                value = 0.5 * (old[:, at] + land[:, at]) - LEARN_RATE * item_sum[slot]
                out[:, at] = value
                if tiles is not None:
                    tiles[start + block] = value
            return carry

        lax.fori_loop(0, width // tile // BLEND_GROUP, body, 0)

    groups = slots // FUSED_GROUP

    def pace(j, limit):
        waiter(0, j).wait_send()
        if j + limit < pieces:
            send(0, j + limit)

    def sent(j):
        if wide == window:
            pace(j, window)
            return

        @pl.when(place == 0)
        def _():
            pace(j, wide)

        @pl.when(place != 0)
        def _():
            pace(j, window)

    def rise(j):
        if hops[1] != 0:
            return

        @pl.when(place == 0)
        def _():
            climb(1, j)

        ascend(1, j)

    take_x.wait()
    tiled(x, x_tiles)
    take_y.wait()
    swap.wait()
    tiled(y, y_tiles)
    take_index.wait()
    take_ratings.wait()
    grads(0, groups)
    collect()
    swap = to_partner(grad, grad_land, 1)
    swap.start()
    for j in range(pieces):
        for k in range(j + SIDE if j else 0, min(j + SIDE + 1, pieces)):
            forward(0, k, 0)
        for k in range(j + LOOK if j else 0, min(j + LOOK + 1, pieces)):
            ascend(0, k)
        waiter(0, j).wait_recv()
        sent(j)
        blend(x, land_a, x1, j, x_tiles)
        send(1, j)
        if j >= 1:
            forward(1, j - 1, 0)
            if j <= EARLY:
                rise(j - 1)
        if j == 1:
            swap.wait()
            y[...] = y[...] - LEARN_RATE * (grad[...] + grad_land[...])
            tiled(y, y_tiles)
    late = pieces - EARLY
    each, often = max(1, late // groups), max(1, groups // late)

    def last_grads(g, carry):
        grad_group(g * FUSED_GROUP)

        @pl.when(g == 0)
        def _():
            forward(1, pieces - 1, 0)

        @pl.when(g % often == often - 1)
        def _():
            for k in range(each):
                rise(EARLY + g // often * each + k)

        return carry

    lax.fori_loop(0, groups, last_grads, 0)
    collect()
    other = pl.ds(pl.multiple_of((1 - item) * own, own), own)
    swap = to_partner(grad.at[:, other], part_land, 2)
    swap.start()
    for j in range(pieces):
        waiter(1, j).wait_recv()
        blend(x1, land_b, x_out, j)
    swap.wait()
    y_out[...] = y[:, mine] - LEARN_RATE * (grad[:, mine] + part_land[...])
    for j in range(pieces):
        waiter(1, j).wait_send()
        for flow in range(2):
            forwarded(flow, j)


def handed_over(*blocks):
    count = len(blocks)

    def kernel(*refs):
        sems = refs[-1]
        copies = [
            pltpu.make_async_copy(refs[k], refs[count + k], sems.at[k]) for k in range(count)
        ]
        for copy in copies:
            copy.start()
        for copy in copies:
            copy.wait()

    return pl.pallas_call(
        kernel,
        out_shape=[jax.ShapeDtypeStruct(block.shape, block.dtype) for block in blocks],
        in_specs=[pl.BlockSpec(memory_space=pltpu.VMEM)] * count,
        out_specs=[pl.BlockSpec(memory_space=pl.ANY)] * count,
        scratch_shapes=[pltpu.SemaphoreType.DMA((count,))],
        compiler_params=pltpu.CompilerParams(vmem_limit_bytes=8 << 20),
    )(*blocks)


def two_steps_fused(hops, item_here, user_here, slot_values, row_index, column_index, block_total):
    rank, items = item_here.shape
    slots, tile = slot_values.shape[0], slot_values.shape[-1]
    own = user_here.shape[1]
    users = own * lax.axis_size("item")
    lines = 4 + -(-items // (tile * slots)) + -(-users // (tile * slots))
    lines = -(-lines // 8) * 8
    scalars = pl.BlockSpec(memory_space=pltpu.SMEM)
    whole = pl.BlockSpec(memory_space=pltpu.VMEM)
    anywhere = pl.BlockSpec(memory_space=pl.ANY)
    held = lambda *shape: pltpu.VMEM(shape, jnp.float32)
    relay = held(PIECES, rank, items // (PIECES * RELAYS))
    mixed, kept = pl.pallas_call(
        partial(fused_kernel, hops),
        out_shape=[
            jax.ShapeDtypeStruct((rank, items), jnp.float32),
            jax.ShapeDtypeStruct((rank, own), jnp.float32),
        ],
        in_specs=[scalars, whole, whole, anywhere, anywhere, anywhere],
        out_specs=[whole, whole],
        scratch_shapes=[held(rank, items)] * 4
        + [relay, relay]
        + [pltpu.VMEM(slot_values.shape, slot_values.dtype)]
        + [held(slots + 1, rank, tile)] * 2
        + [held(rank, users)] * 3
        + [held(rank, own), held(items // tile, rank, tile), held(users // tile, rank, tile)]
        + [pltpu.VMEM((lines, slots), jnp.int32), pltpu.SMEM((lines, slots), jnp.int32)]
        + [pltpu.SemaphoreType.DMA((PIECES,))] * 8
        + [pltpu.SemaphoreType.DMA((6,)), pltpu.SemaphoreType.DMA((4,))],
        compiler_params=pltpu.CompilerParams(
            collective_id=1 + hops[0], has_side_effects=True, vmem_limit_bytes=48 << 20
        ),
        cost_estimate=pl.CostEstimate(
            flops=20 * slots * tile * tile * rank,
            bytes_accessed=16 * rank * items,
            transcendentals=0,
        ),
    )(block_total, row_index[None], column_index[None], item_here, user_here, slot_values)
    return handed_over(mixed, kept)


def per_device(item_factors, user_factors, ratings, block_rows, block_cols, block_count, hop_steps):
    mixed = lambda pair: (
        1 not in pair
        and lax.axis_size("item") == 2
        and lax.axis_size("site") % RELAYS == 0
        and lax.axis_size("site") > 2 * RELAYS
    )
    weights = jnp.array([HOPS, 1], jnp.int32)
    chosen = jnp.sum(hop_steps * weights) - 1
    pairs = [divmod(code, HOPS) for code in range(1, HOPS * HOPS - 1)]
    item_here, user_here = lax.switch(
        chosen,
        [partial(two_steps_fused if mixed(pair) else two_steps, pair) for pair in pairs],
        item_factors[0],
        user_factors[0],
        ratings[0, 0],
        block_rows[0, 0],
        block_cols[0, 0],
        block_count[0],
    )
    return (item_here[None], user_here[None])


def solution(mesh):
    return jax.shard_map(
        per_device,
        mesh=mesh,
        in_specs=(
            P("site", None, "item"),
            P("site", None, "item"),
            P("site", "item", None, None, None),
            P("site", "item", None),
            P("site", "item", None),
            P("site", "item"),
            P(),
        ),
        out_specs=(P("site", None, "item"), P("site", None, "item")),
        check_vma=False,
    )
```

```python
from functools import partial

import jax
import jax.numpy as jnp
from jax import lax
from jax.experimental import pallas as pl
from jax.experimental.pallas import tpu as pltpu
from jax.sharding import PartitionSpec as P

ITERS = 2
HOPS = 3
LEARN_RATE = 0.05
CHUNKS = 4
GROUP = 8
RELAYS = 4
KERNEL_WEIGHT = 450
PIECES = 16
FUSED_GROUP = 16
WINDOW = 3
LOOK = 2
SIDE = 2
EARLY = 12
BLEND_GROUP = 8
BLEND_STEPS = 8


def passed_along(block, axis, distance):
    devices = range(lax.axis_size(axis))
    route = [((i - distance) % len(devices), i) for i in devices]
    return lax.ppermute(block, axis, route)


def split_high_low(values):
    high = values.astype(jnp.bfloat16)
    low = (values - high.astype(jnp.float32)).astype(jnp.bfloat16)
    return high, low


def dot_f32(lhs, rhs, lhs_dim, rhs_dim):
    return lax.dot_general(
        lhs, rhs, (((lhs_dim,), (rhs_dim,)), ((), ())), preferred_element_type=jnp.float32
    )


def grads_kernel(chunks, rows_ref, cols_ref, count_ref, *refs):
    x_refs = refs[:chunks]
    y_ref, ratings_ref = refs[chunks : chunks + 2]
    base_ref, user_ref = refs[chunks + 2 :]
    group, tile = ratings_ref.shape[0], ratings_ref.shape[-1]
    rank = y_ref.shape[0]
    first = pl.program_id(0) * group
    total = count_ref[0]

    @pl.when(pl.program_id(0) == 0)
    def _():
        start = 0
        for x_ref in x_refs:
            base_ref[start : start + x_ref.shape[0], :] = 0.5 * x_ref[...]
            start += x_ref.shape[0]
        user_ref[...] = jnp.zeros_like(user_ref)

    @pl.when(first < total)
    def _():
        parts = []
        for k in range(group):
            row = pl.ds(pl.multiple_of(rows_ref[first + k] * tile, tile), tile)
            col = pl.ds(pl.multiple_of(cols_ref[first + k] * tile, tile), tile)
            limit = jnp.where(first + k < total, 1.0, 0.0).astype(jnp.float32)
            x = jnp.concatenate([x_ref[:, row] for x_ref in x_refs], axis=0)
            x_high, x_low = split_high_low(x)
            y_high, y_low = split_high_low(y_ref[:, col])
            rebuilt = dot_f32(
                jnp.concatenate([x_high, x_low, x_high], axis=0),
                jnp.concatenate([y_high, y_high, y_low], axis=0),
                0,
                0,
            )
            clipped = jnp.clip(rebuilt - ratings_ref[k].astype(jnp.float32), -limit, limit)
            c_high, c_low = split_high_low(clipped)
            item_pair = dot_f32(jnp.concatenate([y_high, y_low], axis=0), c_high, 1, 1)
            item_part = item_pair[:rank] + item_pair[rank:] + dot_f32(y_high, c_low, 1, 1)
            user_pair = dot_f32(jnp.concatenate([x_high, x_low], axis=0), c_high, 1, 0)
            user_part = user_pair[:rank] + user_pair[rank:] + dot_f32(x_high, c_low, 1, 0)
            parts.append((row, col, item_part, user_part))
        for row, col, item_part, user_part in parts:
            base_ref[:, row] -= LEARN_RATE * item_part
            user_ref[:, col] += user_part


def local_grads(x_parts, users_whole, slot_values, row_index, column_index, block_total):
    chunks = len(x_parts)
    slot_total, tile = slot_values.shape[0], slot_values.shape[-1]
    rank, users = users_whole.shape
    items = x_parts[0].shape[1]
    once = pl.Buffered(1)
    held = lambda shape: pl.BlockSpec(shape, lambda i, *_: (0, 0), pipeline_mode=once)
    return pl.pallas_call(
        partial(grads_kernel, chunks),
        grid_spec=pltpu.PrefetchScalarGridSpec(
            num_scalar_prefetch=3,
            grid=(slot_total // GROUP,),
            in_specs=[held(part.shape) for part in x_parts]
            + [held((rank, users)), pl.BlockSpec((GROUP, tile, tile), lambda i, *_: (i, 0, 0))],
            out_specs=[held((rank, items)), held((rank, users))],
        ),
        out_shape=[
            jax.ShapeDtypeStruct((rank, items), jnp.float32),
            jax.ShapeDtypeStruct((rank, users), jnp.float32),
        ],
        compiler_params=pltpu.CompilerParams(vmem_limit_bytes=24 << 20),
        cost_estimate=pl.CostEstimate(
            flops=KERNEL_WEIGHT * slot_total * tile * tile * rank,
            bytes_accessed=8 * rank * items + 2 * slot_total * tile * tile,
            transcendentals=0,
        ),
    )(row_index, column_index, block_total, *x_parts, users_whole, slot_values)


def over_items(block):
    total = block
    for distance in range(1, lax.axis_size("item")):
        total = total + passed_along(block, "item", distance)
    return total


def owned_part(whole):
    count = lax.axis_size("item")
    width = whole.shape[1] // count
    me = lax.axis_index("item")
    cut = lambda who: lax.dynamic_slice_in_dim(whole, who * width, width, axis=1)
    total = cut(me)
    for distance in range(1, count):
        total = total + passed_along(cut(lax.rem(me + distance, count)), "item", distance)
    return total


def kept_part(whole):
    width = whole.shape[1] // lax.axis_size("item")
    return lax.dynamic_slice_in_dim(whole, lax.axis_index("item") * width, width, axis=1)


def blend_kernel(base_ref, *refs):
    out_ref = refs[-1]
    start = 0
    for ref in refs[:-1]:
        rows = slice(start, start + ref.shape[0])
        out_ref[rows, :] = base_ref[rows, :] + 0.5 * ref[...]
        start += ref.shape[0]


def blend(base, peers):
    rank, items = base.shape
    width = items // BLEND_STEPS
    spec = lambda rows: pl.BlockSpec((rows, width), lambda i: (0, i))
    return pl.pallas_call(
        blend_kernel,
        grid=(BLEND_STEPS,),
        in_specs=[spec(rank)] + [spec(peer.shape[0]) for peer in peers],
        out_specs=spec(rank),
        out_shape=jax.ShapeDtypeStruct((rank, items), jnp.float32),
    )(base, *peers)


def cut_rows(block):
    size = block.shape[0] // CHUNKS
    return [block[c * size : (c + 1) * size] for c in range(CHUNKS)]


def two_steps(hops, item_here, user_here, slot_values, row_index, column_index, block_total):
    grads = lambda parts, users: local_grads(
        parts, users, slot_values, row_index, column_index, block_total
    )
    peers = [passed_along(part, "site", -(1 << hops[0])) for part in cut_rows(item_here)]
    users_whole = lax.all_gather(user_here, "item", axis=1, tiled=True)
    base, user_grad = grads([item_here], users_whole)
    users_whole = users_whole - LEARN_RATE * over_items(user_grad)
    x_parts = [part + 0.5 * peer for part, peer in zip(cut_rows(base), peers)]
    peers = [passed_along(part, "site", -(1 << hops[1])) for part in x_parts]
    base, user_grad = grads(x_parts, users_whole)
    return blend(base, peers), kept_part(users_whole) - LEARN_RATE * owned_part(user_grad)


def strongest(values):
    while values.shape[0] > 1:
        half = values.shape[0] // 2
        values = jnp.maximum(values[:half], values[half:])
    return values


def slot_links(keys, blocks):
    slots = keys.shape[1]
    here = jnp.broadcast_to(keys, (slots, slots))
    there = here.T
    slot = lax.broadcasted_iota(jnp.int32, (slots, slots), 0)
    lane = lax.broadcasted_iota(jnp.int32, (slots, slots), 1)

    def latest(hit):
        found = strongest(jnp.where(hit, slot, -1))
        return jnp.where(found < 0, slots, found)

    before = latest(jnp.logical_and(there == here, slot < lane))
    return [before] + [latest(there == lane + start) for start in range(0, blocks, slots)]


def fused_kernel(hops, count_ref, rows_in, cols_in, x_in, y_in, ratings_in, x_out, y_out, *refs):
    x, x1, land_a, land_b, relay_a, relay_b, ratings, item_sum, user_sum = refs[:9]
    y, grad, grad_land, part_land, x_tiles, y_tiles = refs[9:15]
    links, index = refs[15:17]
    send_a, recv_a, send_b, recv_b, take_a, give_a, take_b, give_b, swaps, loads = refs[17:]
    site, item = lax.axis_index("site"), lax.axis_index("item")
    sites = lax.axis_size("site")
    place = lax.rem(site, RELAYS)
    layer = site - place
    last = RELAYS - 1
    ahead = lax.rem(site + sites - RELAYS, sites)
    behind = lax.rem(site + RELAYS, sites)
    ahead_layer, behind_layer = ahead - place, behind - place
    rank, items = x.shape
    own = y_in.shape[1]
    users = y.shape[1]
    slots, tile = ratings.shape[0], ratings.shape[-1]
    row_blocks, column_blocks = items // tile, users // tile
    pieces = PIECES
    width = items // pieces
    part = width // RELAYS
    at_row_last = 3
    at_col_prev = at_row_last + -(-row_blocks // slots)
    at_col_last = at_col_prev + 1

    def view(ref, j):
        return ref.at[:, pl.ds(pl.multiple_of(j * width, tile), width)]

    def slab(ref, j, q, count=1):
        return ref.at[:, pl.ds(pl.multiple_of(j * width + q * part, tile), count * part)]

    def copy(src, dst, send, recv, target):
        return pltpu.make_async_remote_copy(
            src_ref=src,
            dst_ref=dst,
            send_sem=send,
            recv_sem=recv,
            device_id=(item, target),
            device_id_type=pl.DeviceIdType.MESH,
        )

    def to_partner(src, dst, k):
        return pltpu.make_async_remote_copy(
            src_ref=src,
            dst_ref=dst,
            send_sem=swaps.at[2 * k],
            recv_sem=swaps.at[2 * k + 1],
            device_id=(1 - item, site),
            device_id_type=pl.DeviceIdType.MESH,
        )

    flows = (
        (hops[0], x_in, land_a, relay_a, send_a, recv_a, take_a, give_a),
        (hops[1], x1, land_b, relay_b, send_b, recv_b, take_b, give_b),
    )

    def send(flow, j):
        hop, src, land, relay, send_sem, recv_sem, take, give = flows[flow]
        if hop != 0:
            copy(view(src, j), view(land, j), send_sem.at[j], recv_sem.at[j], ahead).start()
            return
        for here in range(1, RELAYS):

            @pl.when(place == here)
            def _():
                count = last if here == 2 else RELAYS
                copy(
                    slab(src, j, 0, count),
                    slab(land, j, 0, count),
                    send_sem.at[j],
                    recv_sem.at[j],
                    site - 1,
                ).start()
                if here == 2:
                    copy(
                        slab(src, j, last), relay.at[j], send_sem.at[j], take.at[j], site - 2
                    ).start()

        @pl.when(place == 0)
        def _():
            for q in range(last, 0, -1):
                copy(slab(src, j, q), relay.at[j], send_sem.at[j], take.at[j], site + q).start()
            if flow == 0:
                climb(flow, j)

    def climb(flow, j):
        hop, src, land, relay, send_sem, recv_sem, take, give = flows[flow]
        copy(
            slab(src, j, 0), slab(land, j, 0), send_sem.at[j], recv_sem.at[j], ahead + last
        ).start()

    def forward(flow, j, here):
        hop, src, land, relay, send_sem, recv_sem, take, give = flows[flow]
        if hop != 0:
            return

        @pl.when(place == here)
        def _():
            q, target = (last, layer + 1) if here == 0 else (here, ahead_layer + last)
            copy(relay.at[j], relay.at[j], give.at[j], take.at[j], ahead).wait_recv()
            copy(relay.at[j], slab(land, j, q), give.at[j], recv_sem.at[j], target).start()

    def ascend(flow, j):
        for here in range(1, RELAYS):
            forward(flow, j, here)

    def forwarded(flow, j):
        hop, src, land, relay, send_sem, recv_sem, take, give = flows[flow]
        if hop != 0:
            return

        copy(relay.at[j], relay.at[j], give.at[j], take.at[j], ahead).wait_send()

    def waiter(flow, j):
        hop, src, land, relay, send_sem, recv_sem, take, give = flows[flow]
        return copy(view(src, j), view(land, j), send_sem.at[j], recv_sem.at[j], ahead)

    mine = pl.ds(pl.multiple_of(item * own, own), own)
    take_x = pltpu.make_async_copy(x_in, x, loads.at[0])
    take_y = pltpu.make_async_copy(y_in, y.at[:, mine], loads.at[1])
    take_ratings = pltpu.make_async_copy(ratings_in, ratings, loads.at[2])
    take_x.start()
    take_y.start()
    take_ratings.start()
    barrier = pltpu.get_barrier_semaphore()

    def greet(core, peer):
        pl.semaphore_signal(
            barrier, inc=1, device_id=(core, peer), device_id_type=pl.DeviceIdType.MESH
        )

    for k in range(1, RELAYS):
        greet(item, layer + lax.rem(place + k, RELAYS))
    greet(item, ahead)
    greet(item, behind)
    greet(1 - item, site)

    @pl.when(place != last)
    def _():
        greet(item, ahead_layer + last)
        pl.semaphore_wait(barrier, RELAYS + 3)

    @pl.when(place == last)
    def _():
        for q in range(last):
            greet(item, behind_layer + q)
        pl.semaphore_wait(barrier, RELAYS + 2 + last)

    swap = to_partner(y_in, y.at[:, mine], 0)
    swap.start()
    window = min(WINDOW, pieces)

    def open_flow(j, carry):
        send(0, j)
        return carry

    lax.fori_loop(0, window, open_flow, 0)
    row_links = slot_links(rows_in[...], row_blocks)
    col_links = slot_links(cols_in[...], column_blocks)
    lines = [rows_in[...], cols_in[...]] + row_links + col_links
    for at, line in enumerate(lines):
        links[at : at + 1, :] = line
    take_index = pltpu.make_async_copy(links, index, loads.at[3])
    take_index.start()
    item_sum[slots] = jnp.zeros((rank, tile), jnp.float32)
    user_sum[slots] = jnp.zeros((rank, tile), jnp.float32)
    def tiled(src, dst):
        def body(c, carry):
            dst[c] = src[:, pl.ds(pl.multiple_of(c * tile, tile), tile)]
            return carry

        lax.fori_loop(0, dst.shape[0], body, 0, unroll=8)

    total = count_ref[0]

    def grad_group(first):
        parts = []
        for k in range(FUSED_GROUP):
            slot = first + k
            limit = jnp.clip(total - slot, 0, 1).astype(jnp.float32)
            x_high, x_low = split_high_low(x_tiles[index[0, slot]])
            y_high, y_low = split_high_low(y_tiles[index[1, slot]])
            rebuilt = dot_f32(
                jnp.concatenate([x_high, x_low, x_high], axis=0),
                jnp.concatenate([y_high, y_high, y_low], axis=0),
                0,
                0,
            )
            clipped = jnp.clip(rebuilt - ratings[slot].astype(jnp.float32), -limit, limit)
            c_high, c_low = split_high_low(clipped)
            item_part = dot_f32(
                jnp.concatenate([y_high, y_low, y_high], axis=1),
                jnp.concatenate([c_high, c_high, c_low], axis=1),
                1,
                1,
            )
            user_part = dot_f32(
                jnp.concatenate([x_high, x_low, x_high], axis=1),
                jnp.concatenate([c_high, c_high, c_low], axis=0),
                1,
                0,
            )
            parts.append((slot, item_part, user_part))
        for slot, item_part, user_part in parts:
            item_sum[slot] = item_part + item_sum[index[2, slot]]
            user_sum[slot] = user_part + user_sum[index[at_col_prev, slot]]

    def grads(start, stop):
        def body(g, carry):
            grad_group(g * FUSED_GROUP)
            return carry

        lax.fori_loop(start, stop, body, 0)

    def collect():
        def body(c, carry):
            at = pl.ds(pl.multiple_of(c * tile, tile), tile)
            grad[:, at] = user_sum[index[at_col_last, c]]
            return carry

        lax.fori_loop(0, column_blocks, body, 0)

    def blend(old, land, out, j, tiles=None):
        start = j * width // tile
        line, lane = at_row_last + start // slots, start % slots

        def body(g, carry):
            for k in range(BLEND_GROUP):
                block = g * BLEND_GROUP + k
                at = pl.ds(pl.multiple_of((start + block) * tile, tile), tile)
                slot = index[line, lane + block]
                value = 0.5 * (old[:, at] + land[:, at]) - LEARN_RATE * item_sum[slot]
                out[:, at] = value
                if tiles is not None:
                    tiles[start + block] = value
            return carry

        lax.fori_loop(0, width // tile // BLEND_GROUP, body, 0)

    groups = slots // FUSED_GROUP

    def each(start, stop, step):
        def body(j, carry):
            step(j)
            return carry

        lax.fori_loop(start, stop, body, 0)

    def ahead_of(first, step):
        def body(j):
            pl.when(j + first < pieces)(lambda: step(j + first))

        return body

    def first_step(j):
        ahead_of(SIDE, lambda k: forward(0, k, 0))(j)
        ahead_of(LOOK, lambda k: ascend(0, k))(j)
        waiter(0, j).wait_recv()
        waiter(0, j).wait_send()
        ahead_of(window, lambda k: send(0, k))(j)
        blend(x, land_a, x1, j, x_tiles)
        send(1, j)

        @pl.when(j >= 1)
        def _():
            forward(1, j - 1, 0)
            pl.when(j <= EARLY)(lambda: rise(j - 1))

        @pl.when(j == 1)
        def _():
            swap.wait()
            y[...] = y[...] - LEARN_RATE * (grad[...] + grad_land[...])
            tiled(y, y_tiles)

    def second_step(j):
        waiter(1, j).wait_recv()
        blend(x1, land_b, x_out, j)

    def settle(j):
        waiter(1, j).wait_send()
        for flow in range(2):
            forwarded(flow, j)

    def rise(j):
        if hops[1] != 0:
            return

        @pl.when(place == 0)
        def _():
            climb(1, j)

        ascend(1, j)

    take_x.wait()
    tiled(x, x_tiles)
    take_y.wait()
    swap.wait()
    tiled(y, y_tiles)
    take_index.wait()
    take_ratings.wait()
    grads(0, groups)
    collect()
    swap = to_partner(grad, grad_land, 1)
    swap.start()
    each(0, min(SIDE, pieces), lambda k: forward(0, k, 0))
    each(0, min(LOOK, pieces), lambda k: ascend(0, k))
    each(0, pieces, first_step)
    late = pieces - EARLY
    batch, often = max(1, late // groups), max(1, groups // late)

    def last_grads(g):
        grad_group(g * FUSED_GROUP)

        @pl.when(g == 0)
        def _():
            forward(1, pieces - 1, 0)

        @pl.when(g % often == often - 1)
        def _():
            for k in range(batch):
                rise(EARLY + g // often * batch + k)

    each(0, groups, last_grads)
    collect()
    other = pl.ds(pl.multiple_of((1 - item) * own, own), own)
    swap = to_partner(grad.at[:, other], part_land, 2)
    swap.start()
    each(0, pieces, second_step)
    swap.wait()
    y_out[...] = y[:, mine] - LEARN_RATE * (grad[:, mine] + part_land[...])
    each(0, pieces, settle)


def handed_over(*blocks):
    count = len(blocks)

    def kernel(*refs):
        sems = refs[-1]
        copies = [
            pltpu.make_async_copy(refs[k], refs[count + k], sems.at[k]) for k in range(count)
        ]
        for copy in copies:
            copy.start()
        for copy in copies:
            copy.wait()

    return pl.pallas_call(
        kernel,
        out_shape=[jax.ShapeDtypeStruct(block.shape, block.dtype) for block in blocks],
        in_specs=[pl.BlockSpec(memory_space=pltpu.VMEM)] * count,
        out_specs=[pl.BlockSpec(memory_space=pl.ANY)] * count,
        scratch_shapes=[pltpu.SemaphoreType.DMA((count,))],
        compiler_params=pltpu.CompilerParams(vmem_limit_bytes=8 << 20),
    )(*blocks)


def two_steps_fused(hops, item_here, user_here, slot_values, row_index, column_index, block_total):
    rank, items = item_here.shape
    slots, tile = slot_values.shape[0], slot_values.shape[-1]
    own = user_here.shape[1]
    users = own * lax.axis_size("item")
    lines = 4 + -(-items // (tile * slots)) + -(-users // (tile * slots))
    lines = -(-lines // 8) * 8
    scalars = pl.BlockSpec(memory_space=pltpu.SMEM)
    whole = pl.BlockSpec(memory_space=pltpu.VMEM)
    anywhere = pl.BlockSpec(memory_space=pl.ANY)
    held = lambda *shape: pltpu.VMEM(shape, jnp.float32)
    relay = held(PIECES, rank, items // (PIECES * RELAYS))
    mixed, kept = pl.pallas_call(
        partial(fused_kernel, hops),
        out_shape=[
            jax.ShapeDtypeStruct((rank, items), jnp.float32),
            jax.ShapeDtypeStruct((rank, own), jnp.float32),
        ],
        in_specs=[scalars, whole, whole, anywhere, anywhere, anywhere],
        out_specs=[whole, whole],
        scratch_shapes=[held(rank, items)] * 4
        + [relay, relay]
        + [pltpu.VMEM(slot_values.shape, slot_values.dtype)]
        + [held(slots + 1, rank, tile)] * 2
        + [held(rank, users)] * 3
        + [held(rank, own), held(items // tile, rank, tile), held(users // tile, rank, tile)]
        + [pltpu.VMEM((lines, slots), jnp.int32), pltpu.SMEM((lines, slots), jnp.int32)]
        + [pltpu.SemaphoreType.DMA((PIECES,))] * 8
        + [pltpu.SemaphoreType.DMA((6,)), pltpu.SemaphoreType.DMA((4,))],
        compiler_params=pltpu.CompilerParams(
            collective_id=1 + hops[0], has_side_effects=True, vmem_limit_bytes=48 << 20
        ),
        cost_estimate=pl.CostEstimate(
            flops=20 * slots * tile * tile * rank,
            bytes_accessed=16 * rank * items,
            transcendentals=0,
        ),
    )(block_total, row_index[None], column_index[None], item_here, user_here, slot_values)
    return handed_over(mixed, kept)


def per_device(item_factors, user_factors, ratings, block_rows, block_cols, block_count, hop_steps):
    mixed = lambda pair: (
        1 not in pair
        and lax.axis_size("item") == 2
        and lax.axis_size("site") % RELAYS == 0
        and lax.axis_size("site") > 2 * RELAYS
    )
    weights = jnp.array([HOPS, 1], jnp.int32)
    chosen = jnp.sum(hop_steps * weights) - 1
    pairs = [divmod(code, HOPS) for code in range(1, HOPS * HOPS - 1)]
    item_here, user_here = lax.switch(
        chosen,
        [partial(two_steps_fused if mixed(pair) else two_steps, pair) for pair in pairs],
        item_factors[0],
        user_factors[0],
        ratings[0, 0],
        block_rows[0, 0],
        block_cols[0, 0],
        block_count[0],
    )
    return (item_here[None], user_here[None])


def solution(mesh):
    return jax.shard_map(
        per_device,
        mesh=mesh,
        in_specs=(
            P("site", None, "item"),
            P("site", None, "item"),
            P("site", "item", None, None, None),
            P("site", "item", None),
            P("site", "item", None),
            P("site", "item"),
            P(),
        ),
        out_specs=(P("site", None, "item"), P("site", None, "item")),
        check_vma=False,
    )
```

```python
from functools import partial

import jax
import jax.numpy as jnp
from jax import lax
from jax.experimental import pallas as pl
from jax.experimental.pallas import tpu as pltpu
from jax.sharding import PartitionSpec as P

ITERS = 2
HOPS = 3
LEARN_RATE = 0.05
CHUNKS = 4
GROUP = 8
RELAYS = 4
KERNEL_WEIGHT = 450
PIECES = 16
FUSED_GROUP = 16
WINDOW = 3
LOOK = 2
SIDE = 2
EARLY = 12
BLEND_GROUP = 8
BLEND_STEPS = 8


def passed_along(block, axis, distance):
    devices = range(lax.axis_size(axis))
    route = [((i - distance) % len(devices), i) for i in devices]
    return lax.ppermute(block, axis, route)


def split_high_low(values):
    high = values.astype(jnp.bfloat16)
    low = (values - high.astype(jnp.float32)).astype(jnp.bfloat16)
    return high, low


def dot_f32(lhs, rhs, lhs_dim, rhs_dim):
    return lax.dot_general(
        lhs, rhs, (((lhs_dim,), (rhs_dim,)), ((), ())), preferred_element_type=jnp.float32
    )


def grads_kernel(chunks, rows_ref, cols_ref, count_ref, *refs):
    x_refs = refs[:chunks]
    y_ref, ratings_ref = refs[chunks : chunks + 2]
    base_ref, user_ref = refs[chunks + 2 :]
    group, tile = ratings_ref.shape[0], ratings_ref.shape[-1]
    rank = y_ref.shape[0]
    first = pl.program_id(0) * group
    total = count_ref[0]

    @pl.when(pl.program_id(0) == 0)
    def _():
        start = 0
        for x_ref in x_refs:
            base_ref[start : start + x_ref.shape[0], :] = 0.5 * x_ref[...]
            start += x_ref.shape[0]
        user_ref[...] = jnp.zeros_like(user_ref)

    @pl.when(first < total)
    def _():
        parts = []
        for k in range(group):
            row = pl.ds(pl.multiple_of(rows_ref[first + k] * tile, tile), tile)
            col = pl.ds(pl.multiple_of(cols_ref[first + k] * tile, tile), tile)
            limit = jnp.where(first + k < total, 1.0, 0.0).astype(jnp.float32)
            x = jnp.concatenate([x_ref[:, row] for x_ref in x_refs], axis=0)
            x_high, x_low = split_high_low(x)
            y_high, y_low = split_high_low(y_ref[:, col])
            rebuilt = dot_f32(
                jnp.concatenate([x_high, x_low, x_high], axis=0),
                jnp.concatenate([y_high, y_high, y_low], axis=0),
                0,
                0,
            )
            clipped = jnp.clip(rebuilt - ratings_ref[k].astype(jnp.float32), -limit, limit)
            c_high, c_low = split_high_low(clipped)
            item_pair = dot_f32(jnp.concatenate([y_high, y_low], axis=0), c_high, 1, 1)
            item_part = item_pair[:rank] + item_pair[rank:] + dot_f32(y_high, c_low, 1, 1)
            user_pair = dot_f32(jnp.concatenate([x_high, x_low], axis=0), c_high, 1, 0)
            user_part = user_pair[:rank] + user_pair[rank:] + dot_f32(x_high, c_low, 1, 0)
            parts.append((row, col, item_part, user_part))
        for row, col, item_part, user_part in parts:
            base_ref[:, row] -= LEARN_RATE * item_part
            user_ref[:, col] += user_part


def local_grads(x_parts, users_whole, slot_values, row_index, column_index, block_total):
    chunks = len(x_parts)
    slot_total, tile = slot_values.shape[0], slot_values.shape[-1]
    rank, users = users_whole.shape
    items = x_parts[0].shape[1]
    once = pl.Buffered(1)
    held = lambda shape: pl.BlockSpec(shape, lambda i, *_: (0, 0), pipeline_mode=once)
    return pl.pallas_call(
        partial(grads_kernel, chunks),
        grid_spec=pltpu.PrefetchScalarGridSpec(
            num_scalar_prefetch=3,
            grid=(slot_total // GROUP,),
            in_specs=[held(part.shape) for part in x_parts]
            + [held((rank, users)), pl.BlockSpec((GROUP, tile, tile), lambda i, *_: (i, 0, 0))],
            out_specs=[held((rank, items)), held((rank, users))],
        ),
        out_shape=[
            jax.ShapeDtypeStruct((rank, items), jnp.float32),
            jax.ShapeDtypeStruct((rank, users), jnp.float32),
        ],
        compiler_params=pltpu.CompilerParams(vmem_limit_bytes=24 << 20),
        cost_estimate=pl.CostEstimate(
            flops=KERNEL_WEIGHT * slot_total * tile * tile * rank,
            bytes_accessed=8 * rank * items + 2 * slot_total * tile * tile,
            transcendentals=0,
        ),
    )(row_index, column_index, block_total, *x_parts, users_whole, slot_values)


def over_items(block):
    total = block
    for distance in range(1, lax.axis_size("item")):
        total = total + passed_along(block, "item", distance)
    return total


def owned_part(whole):
    count = lax.axis_size("item")
    width = whole.shape[1] // count
    me = lax.axis_index("item")
    cut = lambda who: lax.dynamic_slice_in_dim(whole, who * width, width, axis=1)
    total = cut(me)
    for distance in range(1, count):
        total = total + passed_along(cut(lax.rem(me + distance, count)), "item", distance)
    return total


def kept_part(whole):
    width = whole.shape[1] // lax.axis_size("item")
    return lax.dynamic_slice_in_dim(whole, lax.axis_index("item") * width, width, axis=1)


def blend_kernel(base_ref, *refs):
    out_ref = refs[-1]
    start = 0
    for ref in refs[:-1]:
        rows = slice(start, start + ref.shape[0])
        out_ref[rows, :] = base_ref[rows, :] + 0.5 * ref[...]
        start += ref.shape[0]


def blend(base, peers):
    rank, items = base.shape
    width = items // BLEND_STEPS
    spec = lambda rows: pl.BlockSpec((rows, width), lambda i: (0, i))
    return pl.pallas_call(
        blend_kernel,
        grid=(BLEND_STEPS,),
        in_specs=[spec(rank)] + [spec(peer.shape[0]) for peer in peers],
        out_specs=spec(rank),
        out_shape=jax.ShapeDtypeStruct((rank, items), jnp.float32),
    )(base, *peers)


def cut_rows(block):
    size = block.shape[0] // CHUNKS
    return [block[c * size : (c + 1) * size] for c in range(CHUNKS)]


def two_steps(hops, item_here, user_here, slot_values, row_index, column_index, block_total):
    grads = lambda parts, users: local_grads(
        parts, users, slot_values, row_index, column_index, block_total
    )
    peers = [passed_along(part, "site", -(1 << hops[0])) for part in cut_rows(item_here)]
    users_whole = lax.all_gather(user_here, "item", axis=1, tiled=True)
    base, user_grad = grads([item_here], users_whole)
    users_whole = users_whole - LEARN_RATE * over_items(user_grad)
    x_parts = [part + 0.5 * peer for part, peer in zip(cut_rows(base), peers)]
    peers = [passed_along(part, "site", -(1 << hops[1])) for part in x_parts]
    base, user_grad = grads(x_parts, users_whole)
    return blend(base, peers), kept_part(users_whole) - LEARN_RATE * owned_part(user_grad)


def strongest(values):
    while values.shape[0] > 1:
        half = values.shape[0] // 2
        values = jnp.maximum(values[:half], values[half:])
    return values


def slot_links(keys, blocks):
    slots = keys.shape[1]
    here = jnp.broadcast_to(keys, (slots, slots))
    there = here.T
    slot = lax.broadcasted_iota(jnp.int32, (slots, slots), 0)
    lane = lax.broadcasted_iota(jnp.int32, (slots, slots), 1)

    def latest(hit):
        found = strongest(jnp.where(hit, slot, -1))
        return jnp.where(found < 0, slots, found)

    before = latest(jnp.logical_and(there == here, slot < lane))
    return [before] + [latest(there == lane + start) for start in range(0, blocks, slots)]


def fused_kernel(hops, count_ref, rows_in, cols_in, x_in, y_in, ratings_in, x_out, y_out, *refs):
    x, x1, land_a, land_b, relay_a, relay_b, ratings, item_sum, user_sum = refs[:9]
    y, grad, grad_land, part_land, x_tiles, y_tiles = refs[9:15]
    links, index = refs[15:17]
    send_a, recv_a, send_b, recv_b, take_a, give_a, take_b, give_b, swaps, loads = refs[17:]
    site, item = lax.axis_index("site"), lax.axis_index("item")
    sites = lax.axis_size("site")
    place = lax.rem(site, RELAYS)
    layer = site - place
    last = RELAYS - 1
    ahead = lax.rem(site + sites - RELAYS, sites)
    behind = lax.rem(site + RELAYS, sites)
    ahead_layer, behind_layer = ahead - place, behind - place
    rank, items = x.shape
    own = y_in.shape[1]
    users = y.shape[1]
    slots, tile = ratings.shape[0], ratings.shape[-1]
    row_blocks, column_blocks = items // tile, users // tile
    pieces = PIECES
    width = items // pieces
    part = width // RELAYS
    at_row_last = 3
    at_col_prev = at_row_last + -(-row_blocks // slots)
    at_col_last = at_col_prev + 1

    def view(ref, j):
        return ref.at[:, pl.ds(pl.multiple_of(j * width, tile), width)]

    def slab(ref, j, q, count=1):
        return ref.at[:, pl.ds(pl.multiple_of(j * width + q * part, tile), count * part)]

    def copy(src, dst, send, recv, target):
        return pltpu.make_async_remote_copy(
            src_ref=src,
            dst_ref=dst,
            send_sem=send,
            recv_sem=recv,
            device_id=(item, target),
            device_id_type=pl.DeviceIdType.MESH,
        )

    def to_partner(src, dst, k):
        return pltpu.make_async_remote_copy(
            src_ref=src,
            dst_ref=dst,
            send_sem=swaps.at[2 * k],
            recv_sem=swaps.at[2 * k + 1],
            device_id=(1 - item, site),
            device_id_type=pl.DeviceIdType.MESH,
        )

    flows = (
        (hops[0], x_in, land_a, relay_a, send_a, recv_a, take_a, give_a),
        (hops[1], x1, land_b, relay_b, send_b, recv_b, take_b, give_b),
    )

    def send(flow, j):
        hop, src, land, relay, send_sem, recv_sem, take, give = flows[flow]
        if hop != 0:
            copy(view(src, j), view(land, j), send_sem.at[j], recv_sem.at[j], ahead).start()
            return
        for here in range(1, RELAYS):

            @pl.when(place == here)
            def _():
                count = last if here == 2 else RELAYS
                copy(
                    slab(src, j, 0, count),
                    slab(land, j, 0, count),
                    send_sem.at[j],
                    recv_sem.at[j],
                    site - 1,
                ).start()
                if here == 2:
                    copy(
                        slab(src, j, last), relay.at[j], send_sem.at[j], take.at[j], site - 2
                    ).start()

        @pl.when(place == 0)
        def _():
            for q in range(last, 0, -1):
                copy(slab(src, j, q), relay.at[j], send_sem.at[j], take.at[j], site + q).start()
            if flow == 0:
                climb(flow, j)

    def climb(flow, j):
        hop, src, land, relay, send_sem, recv_sem, take, give = flows[flow]
        copy(
            slab(src, j, 0), slab(land, j, 0), send_sem.at[j], recv_sem.at[j], ahead + last
        ).start()

    def forward(flow, j, here):
        hop, src, land, relay, send_sem, recv_sem, take, give = flows[flow]
        if hop != 0:
            return

        @pl.when(place == here)
        def _():
            q, target = (last, layer + 1) if here == 0 else (here, ahead_layer + last)
            copy(relay.at[j], relay.at[j], give.at[j], take.at[j], ahead).wait_recv()
            copy(relay.at[j], slab(land, j, q), give.at[j], recv_sem.at[j], target).start()

    def ascend(flow, j):
        for here in range(1, RELAYS):
            forward(flow, j, here)

    def forwarded(flow, j):
        hop, src, land, relay, send_sem, recv_sem, take, give = flows[flow]
        if hop != 0:
            return

        copy(relay.at[j], relay.at[j], give.at[j], take.at[j], ahead).wait_send()

    def waiter(flow, j):
        hop, src, land, relay, send_sem, recv_sem, take, give = flows[flow]
        return copy(view(src, j), view(land, j), send_sem.at[j], recv_sem.at[j], ahead)

    mine = pl.ds(pl.multiple_of(item * own, own), own)
    take_x = pltpu.make_async_copy(x_in, x, loads.at[0])
    take_y = pltpu.make_async_copy(y_in, y.at[:, mine], loads.at[1])
    take_ratings = pltpu.make_async_copy(ratings_in, ratings, loads.at[2])
    take_x.start()
    take_y.start()
    take_ratings.start()
    barrier = pltpu.get_barrier_semaphore()

    def greet(core, peer):
        pl.semaphore_signal(
            barrier, inc=1, device_id=(core, peer), device_id_type=pl.DeviceIdType.MESH
        )

    for k in range(1, RELAYS):
        greet(item, layer + lax.rem(place + k, RELAYS))
    greet(item, ahead)
    greet(item, behind)
    greet(1 - item, site)

    @pl.when(place != last)
    def _():
        greet(item, ahead_layer + last)
        pl.semaphore_wait(barrier, RELAYS + 3)

    @pl.when(place == last)
    def _():
        for q in range(last):
            greet(item, behind_layer + q)
        pl.semaphore_wait(barrier, RELAYS + 2 + last)

    user_swap = to_partner(y_in, y.at[:, mine], 0)
    user_swap.start()
    window = min(WINDOW, pieces)

    def open_flow(j, carry):
        send(0, j)
        return carry

    lax.fori_loop(0, window, open_flow, 0)
    row_links = slot_links(rows_in[...], row_blocks)
    col_links = slot_links(cols_in[...], column_blocks)
    lines = [rows_in[...], cols_in[...]] + row_links + col_links
    for at, line in enumerate(lines):
        links[at : at + 1, :] = line
    take_index = pltpu.make_async_copy(links, index, loads.at[3])
    take_index.start()
    item_sum[slots] = jnp.zeros((rank, tile), jnp.float32)
    user_sum[slots] = jnp.zeros((rank, tile), jnp.float32)
    def tiled(src, dst):
        def body(c, carry):
            dst[c] = src[:, pl.ds(pl.multiple_of(c * tile, tile), tile)]
            return carry

        lax.fori_loop(0, dst.shape[0], body, 0, unroll=8)

    total = count_ref[0]

    def grad_group(first):
        parts = []
        for k in range(FUSED_GROUP):
            slot = first + k
            limit = jnp.clip(total - slot, 0, 1).astype(jnp.float32)
            x_high, x_low = split_high_low(x_tiles[index[0, slot]])
            y_high, y_low = split_high_low(y_tiles[index[1, slot]])
            rebuilt = dot_f32(
                jnp.concatenate([x_high, x_low, x_high], axis=0),
                jnp.concatenate([y_high, y_high, y_low], axis=0),
                0,
                0,
            )
            clipped = jnp.clip(rebuilt - ratings[slot].astype(jnp.float32), -limit, limit)
            c_high, c_low = split_high_low(clipped)
            item_part = dot_f32(
                jnp.concatenate([y_high, y_low, y_high], axis=1),
                jnp.concatenate([c_high, c_high, c_low], axis=1),
                1,
                1,
            )
            user_part = dot_f32(
                jnp.concatenate([x_high, x_low, x_high], axis=1),
                jnp.concatenate([c_high, c_high, c_low], axis=0),
                1,
                0,
            )
            parts.append((slot, item_part, user_part))
        for slot, item_part, user_part in parts:
            item_sum[slot] = item_part + item_sum[index[2, slot]]
            user_sum[slot] = user_part + user_sum[index[at_col_prev, slot]]

    def collect():
        def body(c, carry):
            at = pl.ds(pl.multiple_of(c * tile, tile), tile)
            grad[:, at] = user_sum[index[at_col_last, c]]
            return carry

        lax.fori_loop(0, column_blocks, body, 0)

    def blend(old, land, out, j, tiles=None):
        start = j * width // tile
        line, lane = at_row_last + start // slots, start % slots

        def body(g, carry):
            for k in range(BLEND_GROUP):
                block = g * BLEND_GROUP + k
                at = pl.ds(pl.multiple_of((start + block) * tile, tile), tile)
                slot = index[line, lane + block]
                value = 0.5 * (old[:, at] + land[:, at]) - LEARN_RATE * item_sum[slot]
                out[:, at] = value
                if tiles is not None:
                    tiles[start + block] = value
            return carry

        lax.fori_loop(0, width // tile // BLEND_GROUP, body, 0)

    groups = slots // FUSED_GROUP

    def each(start, stop, step):
        def body(j, carry):
            step(j)
            return carry

        lax.fori_loop(start, stop, body, 0)

    def ahead_of(first, step):
        def body(j):
            pl.when(j + first < pieces)(lambda: step(j + first))

        return body

    def first_step(j):
        ahead_of(SIDE, lambda k: forward(0, k, 0))(j)
        ahead_of(LOOK, lambda k: ascend(0, k))(j)
        waiter(0, j).wait_recv()
        waiter(0, j).wait_send()
        ahead_of(window, lambda k: send(0, k))(j)
        blend(x, land_a, x1, j, x_tiles)
        send(1, j)

        @pl.when(j >= 1)
        def _():
            forward(1, j - 1, 0)
            pl.when(j <= EARLY)(lambda: rise(j - 1))

        @pl.when(j == 1)
        def _():
            swap.wait()
            y[...] = y[...] - LEARN_RATE * (grad[...] + grad_land[...])
            tiled(y, y_tiles)

    def second_step(j):
        waiter(1, j).wait_recv()
        blend(x1, land_b, x_out, j)

    def settle(j):
        waiter(1, j).wait_send()
        for flow in range(2):
            forwarded(flow, j)

    def rise(j):
        if hops[1] != 0:
            return

        @pl.when(place == 0)
        def _():
            climb(1, j)

        ascend(1, j)

    take_x.wait()
    tiled(x, x_tiles)
    take_y.wait()
    user_swap.wait()
    tiled(y, y_tiles)
    take_index.wait()
    take_ratings.wait()
    late = pieces - EARLY
    batch, often = max(1, late // groups), max(1, groups // late)

    def both_grads(phase):
        def grads(g):
            grad_group(g * FUSED_GROUP)

            @pl.when(jnp.logical_and(phase == 1, g == 0))
            def _():
                forward(1, pieces - 1, 0)

            @pl.when(jnp.logical_and(phase == 1, g % often == often - 1))
            def _():
                for k in range(batch):
                    rise(EARLY + g // often * batch + k)

        each(0, groups, grads)
        collect()

        @pl.when(phase == 0)
        def _():
            swap.start()
            each(0, min(SIDE, pieces), lambda k: forward(0, k, 0))
            each(0, min(LOOK, pieces), lambda k: ascend(0, k))
            each(0, pieces, first_step)

    swap = to_partner(grad, grad_land, 1)
    each(0, 2, both_grads)
    other = pl.ds(pl.multiple_of((1 - item) * own, own), own)
    last_swap = to_partner(grad.at[:, other], part_land, 2)
    last_swap.start()
    each(0, pieces, second_step)
    last_swap.wait()
    y_out[...] = y[:, mine] - LEARN_RATE * (grad[:, mine] + part_land[...])
    each(0, pieces, settle)


def handed_over(*blocks):
    count = len(blocks)

    def kernel(*refs):
        sems = refs[-1]
        copies = [
            pltpu.make_async_copy(refs[k], refs[count + k], sems.at[k]) for k in range(count)
        ]
        for copy in copies:
            copy.start()
        for copy in copies:
            copy.wait()

    return pl.pallas_call(
        kernel,
        out_shape=[jax.ShapeDtypeStruct(block.shape, block.dtype) for block in blocks],
        in_specs=[pl.BlockSpec(memory_space=pltpu.VMEM)] * count,
        out_specs=[pl.BlockSpec(memory_space=pl.ANY)] * count,
        scratch_shapes=[pltpu.SemaphoreType.DMA((count,))],
        compiler_params=pltpu.CompilerParams(vmem_limit_bytes=8 << 20),
    )(*blocks)


def two_steps_fused(hops, item_here, user_here, slot_values, row_index, column_index, block_total):
    rank, items = item_here.shape
    slots, tile = slot_values.shape[0], slot_values.shape[-1]
    own = user_here.shape[1]
    users = own * lax.axis_size("item")
    lines = 4 + -(-items // (tile * slots)) + -(-users // (tile * slots))
    lines = -(-lines // 8) * 8
    scalars = pl.BlockSpec(memory_space=pltpu.SMEM)
    whole = pl.BlockSpec(memory_space=pltpu.VMEM)
    anywhere = pl.BlockSpec(memory_space=pl.ANY)
    held = lambda *shape: pltpu.VMEM(shape, jnp.float32)
    relay = held(PIECES, rank, items // (PIECES * RELAYS))
    mixed, kept = pl.pallas_call(
        partial(fused_kernel, hops),
        out_shape=[
            jax.ShapeDtypeStruct((rank, items), jnp.float32),
            jax.ShapeDtypeStruct((rank, own), jnp.float32),
        ],
        in_specs=[scalars, whole, whole, anywhere, anywhere, anywhere],
        out_specs=[whole, whole],
        scratch_shapes=[held(rank, items)] * 4
        + [relay, relay]
        + [pltpu.VMEM(slot_values.shape, slot_values.dtype)]
        + [held(slots + 1, rank, tile)] * 2
        + [held(rank, users)] * 3
        + [held(rank, own), held(items // tile, rank, tile), held(users // tile, rank, tile)]
        + [pltpu.VMEM((lines, slots), jnp.int32), pltpu.SMEM((lines, slots), jnp.int32)]
        + [pltpu.SemaphoreType.DMA((PIECES,))] * 8
        + [pltpu.SemaphoreType.DMA((6,)), pltpu.SemaphoreType.DMA((4,))],
        compiler_params=pltpu.CompilerParams(
            collective_id=1 + hops[0], has_side_effects=True, vmem_limit_bytes=48 << 20
        ),
        cost_estimate=pl.CostEstimate(
            flops=20 * slots * tile * tile * rank,
            bytes_accessed=16 * rank * items,
            transcendentals=0,
        ),
    )(block_total, row_index[None], column_index[None], item_here, user_here, slot_values)
    return handed_over(mixed, kept)


def per_device(item_factors, user_factors, ratings, block_rows, block_cols, block_count, hop_steps):
    mixed = lambda pair: (
        1 not in pair
        and lax.axis_size("item") == 2
        and lax.axis_size("site") % RELAYS == 0
        and lax.axis_size("site") > 2 * RELAYS
    )
    weights = jnp.array([HOPS, 1], jnp.int32)
    chosen = jnp.sum(hop_steps * weights) - 1
    pairs = [divmod(code, HOPS) for code in range(1, HOPS * HOPS - 1)]
    item_here, user_here = lax.switch(
        chosen,
        [partial(two_steps_fused if mixed(pair) else two_steps, pair) for pair in pairs],
        item_factors[0],
        user_factors[0],
        ratings[0, 0],
        block_rows[0, 0],
        block_cols[0, 0],
        block_count[0],
    )
    return (item_here[None], user_here[None])


def solution(mesh):
    return jax.shard_map(
        per_device,
        mesh=mesh,
        in_specs=(
            P("site", None, "item"),
            P("site", None, "item"),
            P("site", "item", None, None, None),
            P("site", "item", None),
            P("site", "item", None),
            P("site", "item"),
            P(),
        ),
        out_specs=(P("site", None, "item"), P("site", None, "item")),
        check_vma=False,
    )
```
